256 devices in a mesh: req: 32 (over z, y), mdl: 8 (over x, core).
Axes of the slice: x: 4, y: 4, z: 8, core: 2. Of those that a mesh axis runs over, the one named last changes fastest.
Arguments:
- tokens: bfloat16 [8192, 2048], P('req', 'mdl'), may hold values from -6 to 6
- prefix_cache: bfloat16 [16384, 2, 2048], P('req', None, 'mdl'), may hold values from -68 to 68
- qkv_weight: bfloat16 [2048, 3, 2048], P(None, None, 'mdl'), may hold values from -0.125 to 0.125
- out_weight: bfloat16 [2048, 2048], P('mdl'), may hold values from -0.75 to 0.75
- gate_up_weight: bfloat16 [2048, 2, 4096], P(None, None, 'mdl'), may hold values from -0.125 to 0.125
- down_weight: bfloat16 [4096, 2048], P('mdl'), may hold values from -0.09375 to 0.09375
- lengths: int32 [128], replicated, may hold values from 0 to 256, as said below
- placement: int32 [128], replicated, may hold values from 0 to 31, as said below
- request_group: int32 [128], replicated, may hold values from 0 to 3
- block_owner: int32 [32], replicated, may hold values from 0 to 31, each once
- start_position: int32 [128], replicated, may hold values from 4096 to 4351
Outputs:
- out: bfloat16 [8192, 2048], P('req', 'mdl')
The draws below stay inside these ranges and needn't reach their ends.
Inputs may be any that keep to these rules, and one draw needn't show every extreme that they name: `placement`: each index of req holds exactly 4 requests. The lengths of the requests on one index of req sum to at most 256, and to exactly 256 on some index; all lengths together sum to exactly 128 times the number of indices of req.
All inputs are finite; a program needn't handle non-finite values.
Results may differ from the reference program's by a relative error of at most 0.017.
Values may be sent and summed in bfloat16 or wider, within the bound.
A program may use at most 128 MiB of HBM per device.

```python
import math
import jax
import jax.numpy as jnp
from jax import lax

D = 2048
H = 16
HD = 128
FF = 4096
G = 4
REQ_DEV = 4
CAP = 256
PB = 512
PREFIX = 4096
R = 128
SLOTS = 8192
N_REQ = 32
N_MDL = 8


def request_layout(key):
    request_count = REQ_DEV * N_REQ
    key_order, key_pair, key_load, key_cut = jax.random.split(jax.random.fold_in(key, 11), 4)
    request_order = jax.random.permutation(key_order, request_count)
    pairing = jax.random.permutation(key_pair, N_REQ)
    heavy_loads = jax.random.randint(key_load, (N_REQ // 2,), CAP // 2, CAP + 1, dtype=jnp.int32)
    heavy_loads = heavy_loads.at[0].set(CAP)
    paired = jnp.concatenate([heavy_loads, CAP - heavy_loads])
    device_loads = jnp.zeros((N_REQ,), jnp.int32).at[pairing].set(paired)
    draws_cut = jax.random.randint(key_cut, (N_REQ, REQ_DEV - 1), 0, 65, dtype=jnp.int32)
    draws_cut = draws_cut.at[pairing[0]].set(0)
    cut_points = jnp.sort(device_loads[:, None] * draws_cut * draws_cut // 4096, axis=1)
    boundaries = jnp.concatenate([jnp.zeros((N_REQ, 1), jnp.int32), cut_points, device_loads[:, None]], axis=1)
    per_device = boundaries[:, 1:] - boundaries[:, :-1]
    holder = jnp.arange(request_count, dtype=jnp.int32) // REQ_DEV
    placement = jnp.zeros((request_count,), jnp.int32).at[request_order].set(holder)
    lengths = jnp.zeros((request_count,), jnp.int32).at[request_order].set(per_device.reshape(-1))
    return (placement, lengths)


def draw_placement(key, part):
    return request_layout(key)[0]


def draw_lengths(key, part):
    return request_layout(key)[1]


def draw_prefix_cache(key, part):
    shape = (N_REQ * PB, 2, D)
    key_base = jax.random.fold_in(jax.random.fold_in(key, 5), 0)
    base = jnp.clip(jax.random.normal(key_base, shape, jnp.float32), -6.0, 6.0)
    return base.astype(jnp.bfloat16)


def place_ends(drawn, stream_key, low, largest):
    longest = drawn.shape.index(max(drawn.shape))
    spots = []
    for shift in (0, 1):
        where = [jax.random.randint(jax.random.fold_in(stream_key, axis), (), 0, length) for axis, length in enumerate(drawn.shape)]
        where[longest] = (where[longest] + shift) % drawn.shape[longest]
        spots.append(tuple(where))
    return drawn.at[spots[0]].set(low).at[spots[1]].set(largest)


def with_spikes(values, own_key, source, target, shards_of, factor):
    def block_of(dim):
        return (jnp.arange(values.shape[dim]) // (values.shape[dim] // shards_of)).reshape((-1,) + (1,) * (values.ndim - 1 - dim))

    one_side = jax.random.permutation(own_key, shards_of)[block_of(target)]
    second = (block_of(target) + shards_of // 2) % shards_of
    return jnp.where((block_of(source) == one_side) | (block_of(source) == second), factor * values, values)


def block_scale(rng, shape, shards, least, top_value):
    level = 1.0
    for dim, blocks in shards:
        steps = jax.random.uniform(jax.random.fold_in(jax.random.fold_in(rng, 6), dim), (blocks,), jnp.float32, least / len(shards), top_value / len(shards))
        level = level * jnp.repeat(jnp.exp(steps), shape[dim] // blocks).reshape((-1,) + (1,) * (len(shape) - 1 - dim))
    return level


def gaussian(key, dims, spread, limit, pieces=(), kind=jnp.bfloat16):
    factor_of = block_scale(key, dims, pieces, -0.22, 0.18) if pieces else 1.0
    drawn = jax.random.normal(key, dims, jnp.float32) * spread * factor_of
    return jnp.minimum(jnp.maximum(drawn, -limit), limit).astype(kind)


def noise_with(own_key, shape, deviation, limit, cuts, heavy, held_as=jnp.bfloat16):
    entries = deviation * jax.random.normal(own_key, shape, jnp.float32)
    if cuts:
        entries = entries * block_scale(own_key, shape, cuts, -0.22, 0.18)
    return jnp.clip(with_spikes(entries, jax.random.fold_in(own_key, 3), *heavy), -limit, limit).astype(held_as)


def setup_inputs(seed: int = 0) -> dict:
    seeds = jax.random.split(jax.random.key(seed), 12)
    return {
        "tokens": gaussian(seeds[0], (SLOTS, D), 1.0, 6.0, ((0, 32), (1, 8))),
        "prefix_cache": draw_prefix_cache(jax.random.fold_in(seeds[11], 71), 0),
        "qkv_weight": gaussian(seeds[2], (D, 3, D), D ** -0.5, 0.125, ((2, 8),)),
        "out_weight": noise_with(seeds[3], (D, D), (D // 16) ** -0.5, 0.75, ((0, 8),), (0, 1, 8, 2.0)),
        "gate_up_weight": gaussian(seeds[4], (D, 2, FF), D ** -0.5, 0.125, ((2, 8),)),
        "down_weight": gaussian(seeds[5], (FF, D), FF ** -0.5, 0.09375, ((0, 8),)),
        "lengths": draw_lengths(jax.random.fold_in(seeds[11], 71), 0),
        "placement": draw_placement(jax.random.fold_in(seeds[11], 71), 0),
        "request_group": place_ends(jax.random.randint(seeds[8], (R,), 0, G), jax.random.fold_in(seeds[8], 1), 0, G - 1).astype(jnp.int32),
        "block_owner": jax.random.permutation(seeds[9], N_REQ).astype(jnp.int32),
        "start_position": place_ends(jax.random.randint(seeds[10], (R,), PREFIX, PREFIX + 256), jax.random.fold_in(seeds[10], 1), PREFIX, (PREFIX + 256) - 1).astype(jnp.int32),
    }


NEG = -1e+30
EPS = 1e-05

def slot_table(lengths, placement, request_group, start_position, device, capacity):
    request_count = lengths.shape[0]
    request_ids = jnp.arange(request_count, dtype=jnp.int32)
    same_device = placement[:, None] == placement[None, :]
    earlier = request_ids[None, :] < request_ids[:, None]
    before = lax.optimization_barrier(jnp.sum(jnp.where(same_device & earlier, lengths[None, :], 0), axis=1)).astype(jnp.int32)
    ending = before + lengths
    slot_ids = jnp.arange(capacity, dtype=jnp.int32)
    belongs = (placement[None, :] == device) & (slot_ids[:, None] >= before[None, :]) & (slot_ids[:, None] < ending[None, :])
    occupied = jnp.any(belongs, axis=1)
    request = lax.optimization_barrier(jnp.sum(jnp.where(belongs, request_ids[None, :], 0), axis=1)).astype(jnp.int32)
    slot_group = jnp.where(occupied, lax.optimization_barrier(jnp.sum(jnp.where(belongs, request_group[None, :], 0), axis=1)), -1).astype(jnp.int32)
    first_slot = lax.optimization_barrier(jnp.sum(jnp.where(belongs, before[None, :], 0), axis=1)).astype(jnp.int32)
    offset = slot_ids - first_slot
    position = lax.optimization_barrier(jnp.sum(jnp.where(belongs, start_position[None, :], 0), axis=1)).astype(jnp.int32) + offset
    return (occupied, request, slot_group, offset, position)

def block_groups(block_owner, group_count):
    block_count = block_owner.shape[0]
    per_group = block_count // group_count
    entry_ids = jnp.arange(block_count, dtype=jnp.int32)
    hits = block_owner[None, :] == entry_ids[:, None]
    entry = lax.optimization_barrier(jnp.sum(jnp.where(hits, entry_ids[None, :], 0), axis=1)).astype(jnp.int32)
    return entry // per_group

def rotate(vectors, position):
    half_width = vectors.shape[-1] // 2
    pair_ids = jnp.arange(half_width, dtype=jnp.float32)
    frequency = jnp.exp(pair_ids * (-2.0 * math.log(10000.0) / vectors.shape[-1]))
    angles = position.astype(jnp.float32)[:, None] * frequency[None, :]
    cosine = jnp.cos(angles)[:, None, :]
    sine_part = jnp.sin(angles)[:, None, :]
    lower = vectors[..., :half_width]
    upper = vectors[..., half_width:]
    return jnp.concatenate([lower * cosine - upper * sine_part, upper * cosine + lower * sine_part], axis=-1)

def layer_norm(values):
    row_mean = lax.optimization_barrier(jnp.mean(values, axis=-1, keepdims=True))
    centered = values - row_mean
    row_var = lax.optimization_barrier(jnp.mean(centered * centered, axis=-1, keepdims=True))
    return centered * lax.rsqrt(row_var + EPS)

def block_partial(queries, key_rows, value_rows, allowed):
    score_scale = queries.shape[-1] ** (-0.5)
    scores = jnp.einsum('shd,khd->hsk', queries.astype(jnp.float32), key_rows.astype(jnp.float32)) * score_scale
    scores = jnp.where(allowed[None], scores, NEG)
    row_max = lax.optimization_barrier(jnp.max(scores, axis=-1))
    weights = jnp.where(allowed[None], jnp.exp(scores - row_max[..., None]), 0.0)
    weight_sum = lax.optimization_barrier(jnp.sum(weights, axis=-1))
    present = jnp.any(allowed, axis=-1)[None, :]
    safe_sum = jnp.where(present, weight_sum, 1.0)
    rounded = lax.optimization_barrier(weights.astype(jnp.bfloat16)).astype(jnp.float32)
    mixture = jnp.einsum('hsk,khd->shd', rounded, value_rows.astype(jnp.float32))
    normalized = (mixture / jnp.transpose(safe_sum)[:, :, None]).astype(jnp.bfloat16)
    log_sum = jnp.where(present, row_max + jnp.log(safe_sum), NEG)
    return (lax.optimization_barrier(normalized), jnp.transpose(log_sum))

def combine(merged, partial_out, partial_lse):
    weighted, running_max, weight_sum = merged
    new_max = jnp.maximum(running_max, partial_lse)
    old_scale = jnp.exp(running_max - new_max)
    new_scale = jnp.exp(partial_lse - new_max)
    weighted = weighted * old_scale[..., None] + partial_out.astype(jnp.float32) * new_scale[..., None]
    return (weighted, new_max, weight_sum * old_scale + new_scale)

def reference(tokens, prefix_cache, qkv_weight, out_weight, gate_up_weight, down_weight, lengths, placement, request_group, block_owner, start_position):
    group_table = block_groups(block_owner, G)
    cached_keys = prefix_cache[:, 0].reshape(N_REQ, PB, H, HD)
    cached_values = prefix_cache[:, 1].reshape(N_REQ, PB, H, HD)
    qkv_matrix = qkv_weight.reshape(D, 3 * D)
    gate_up_matrix = gate_up_weight.reshape(D, 2 * FF)
    out_groups = out_weight.astype(jnp.float32).reshape(N_MDL, D // N_MDL, D)
    down_groups = down_weight.astype(jnp.float32).reshape(N_MDL, FF // N_MDL, D)

    def one_device(device):
        occupied, request, slot_group, offset, position = slot_table(lengths, placement, request_group, start_position, device, CAP)
        slot_rows = lax.dynamic_slice_in_dim(tokens, device * CAP, CAP, 0)
        normed = layer_norm(slot_rows.astype(jnp.float32)).astype(jnp.bfloat16)
        projected = jnp.dot(normed, qkv_matrix, preferred_element_type=jnp.float32).reshape(CAP, 3, H, HD)
        queries = rotate(projected[:, 0], position).astype(jnp.bfloat16)
        key_rows = rotate(projected[:, 1], position).astype(jnp.bfloat16)
        value_rows = projected[:, 2].astype(jnp.bfloat16)
        merged = (jnp.zeros((CAP, H, HD), jnp.float32), jnp.full((CAP, H), NEG, jnp.float32), jnp.zeros((CAP, H), jnp.float32))

        def over_blocks(running, element):
            block_keys, block_values, block_group = element
            allowed = jnp.broadcast_to((slot_group == block_group)[:, None], (CAP, PB))
            partial_out, partial_lse = block_partial(queries, block_keys, block_values, allowed)
            return (combine(running, partial_out, partial_lse), None)
        merged, unused = lax.scan(over_blocks, merged, (cached_keys, cached_values, group_table))
        causal = occupied[:, None] & occupied[None, :] & (request[:, None] == request[None, :]) & (offset[None, :] <= offset[:, None])
        partial_out, partial_lse = block_partial(queries, key_rows, value_rows, causal)
        weighted, running_max, weight_sum = combine(merged, partial_out, partial_lse)
        attention = (weighted / weight_sum[..., None]).reshape(CAP, D).astype(jnp.bfloat16)
        head_terms = jnp.einsum('sgc,gcd->gsd', attention.astype(jnp.float32).reshape(CAP, N_MDL, D // N_MDL), out_groups)
        head_terms = lax.optimization_barrier(head_terms.astype(jnp.bfloat16)).astype(jnp.float32)
        residual = (slot_rows.astype(jnp.float32) + lax.optimization_barrier(jnp.sum(head_terms, axis=0))).astype(jnp.bfloat16)
        normed_two = layer_norm(residual.astype(jnp.float32)).astype(jnp.bfloat16)
        gate_up = jnp.dot(normed_two, gate_up_matrix, preferred_element_type=jnp.float32)
        hidden = (jax.nn.silu(gate_up[:, :FF]) * gate_up[:, FF:]).astype(jnp.bfloat16)
        down_terms = jnp.einsum('sgc,gcd->gsd', hidden.astype(jnp.float32).reshape(CAP, N_MDL, FF // N_MDL), down_groups)
        down_terms = lax.optimization_barrier(down_terms.astype(jnp.bfloat16)).astype(jnp.float32)
        finished = residual.astype(jnp.float32) + lax.optimization_barrier(jnp.sum(down_terms, axis=0))
        return jnp.where(occupied[:, None], finished, 0.0).astype(jnp.bfloat16)
    return lax.map(one_device, jnp.arange(N_REQ, dtype=jnp.int32)).reshape(N_REQ * CAP, D)
```

```python
import functools
import math

import jax
import jax.numpy as jnp
from jax import lax
from jax.experimental import pallas as pl
from jax.experimental.pallas import tpu as pltpu
from jax.sharding import PartitionSpec as P

HD = 128
NEG = -1e30
EPS = 1e-05
NX, NY, NZ = 4, 4, 8
MESH = pl.DeviceIdType.MESH
F32 = jnp.float32
BF16 = jnp.bfloat16


def dot(a, b):
    return jnp.dot(a, b, preferred_element_type=F32)


def layer_kernel(
    tok, kc, vc, lens, place, group, start, owner, wqkv, wo, wg, wu, wd,
    out,
    tokg, resg, normed, wqkv_v, wo_v, wg_v, wu_v, wd_v,
    kbuf, vtbuf, qbuf, kloc, vtloc, s_scr, part_acc, part_stat, suf_acc, suf_stat,
    rin_acc, rin_stat, rout_acc, rout_stat, grp_scr, bg_scr,
    pair_out, pair_in, stage, ain, lin, rin, mine, res_own,
    wsem, kv_s, kv_r, q_s, q_r, ra_s, ra_r, rs_s, rs_r,
    ag_s, ag_r, sc_s, sc_r,
):
    cap = tok.shape[0]
    width = tok.shape[1]
    req = lax.axis_index("req")
    mdl = lax.axis_index("mdl")
    z = req // NY
    y = req % NY
    x = mdl // 2
    c = mdl % 2
    xr, xl, xa = (x + 1) % NX, (x + NX - 1) % NX, (x + 2) % NX
    yr, yl, ya = (y + 1) % NY, (y + NY - 1) % NY, (y + 2) % NY
    zr, zl = (z + 1) % NZ, (z + NZ - 1) % NZ
    sib = (req, x * 2 + (1 - c))
    x_right = (req, xr * 2 + c)
    x_left = (req, xl * 2 + c)
    y_right = (z * NY + yr, mdl)
    y_left = (z * NY + yl, mdl)
    z_right = (zr * NY + y, mdl)
    z_left = (zl * NY + y, mdl)
    pending = []

    def send(src, dst, s_sem, r_sem, device):
        copy = pltpu.make_async_remote_copy(
            src_ref=src, dst_ref=dst, send_sem=s_sem, recv_sem=r_sem,
            device_id=device, device_id_type=MESH,
        )
        copy.start()
        pending.append(copy)
        return copy

    loads = []
    for i, (src, dst) in enumerate(
        ((wqkv, wqkv_v), (wo, wo_v), (wg, wg_v), (wu, wu_v), (wd, wd_v))
    ):
        load = pltpu.make_async_copy(src, dst, wsem.at[i])
        load.start()
        loads.append(load)

    barrier = pltpu.get_barrier_semaphore()
    for device in (sib, x_right, x_left, y_right, y_left, z_right, z_left):
        pl.semaphore_signal(barrier, inc=1, device_id=device, device_id_type=MESH)
    pl.semaphore_wait(barrier, 7)

    class Gather:
        def __init__(self, buf, n):
            self.buf, self.n = buf, n
            s, r = ag_s.at[n], ag_r.at[n]
            self.s, self.r = s, r
            own = buf.at[mdl]
            self.c_right = send(own, own, s.at[0], r.at[0], x_right)
            self.c_left = send(own, own, s.at[1], r.at[1], x_left)
            self.c_sib = send(own, own, s.at[2], r.at[2], sib)

        def finish(self):
            buf, s, r = self.buf, self.s, self.r
            half = cap // 2
            from_left, from_right, far = xl * 2 + c, xr * 2 + c, xa * 2 + c
            low, high = pl.ds(0, half), pl.ds(half, half)
            self.c_right.wait_recv()
            f_right = send(buf.at[from_left, low], buf.at[from_left, low], s.at[3], r.at[3], x_right)
            s_left = send(buf.at[from_left], buf.at[from_left], s.at[4], r.at[4], sib)
            self.c_left.wait_recv()
            f_left = send(buf.at[from_right, high], buf.at[from_right, high], s.at[5], r.at[5], x_left)
            s_right = send(buf.at[from_right], buf.at[from_right], s.at[6], r.at[6], sib)
            f_right.wait_recv()
            s_low = send(buf.at[far, low], buf.at[far, low], s.at[7], r.at[7], sib)
            f_left.wait_recv()
            s_high = send(buf.at[far, high], buf.at[far, high], s.at[8], r.at[8], sib)
            for copy in (self.c_sib, s_left, s_right, s_low, s_high):
                copy.wait_recv()

    def reduce_scatter(n, chunk):
        half = cap // 2
        low, high = pl.ds(0, half), pl.ds(half, half)
        s, r = sc_s.at[n], sc_r.at[n]
        order = (xa, xr, xl, x)
        pairs = []
        for i, xd in enumerate(order):
            pair_out[n, i] = chunk(xd * 2 + (1 - c)).astype(BF16)
            pairs.append(send(pair_out.at[n, i], pair_in.at[n, i], s.at[i], r.at[i], sib))

        def combined(i):
            own = chunk(order[i] * 2 + c)
            pairs[i].wait_recv()
            return own + pair_in[n, i].astype(F32)

        stage[n, 0] = combined(0).astype(BF16)
        a_low = send(stage.at[n, 0, low], ain.at[n, low], s.at[4], r.at[4], x_right)
        a_high = send(stage.at[n, 0, high], ain.at[n, high], s.at[5], r.at[5], x_left)
        to_right = combined(1)
        mine[0] = to_right[:half]
        stage[n, 1, high] = to_right[half:].astype(BF16)
        b_high = send(stage.at[n, 1, high], lin.at[n, high], s.at[6], r.at[6], x_right)
        to_left = combined(2)
        mine[1] = to_left[half:]
        stage[n, 2, low] = to_left[:half].astype(BF16)
        b_low = send(stage.at[n, 2, low], rin.at[n, low], s.at[7], r.at[7], x_left)
        own = combined(3)
        mine[2] = own[:half]
        mine[3] = own[half:]
        a_low.wait_recv()
        stage[n, 1, low] = (mine[0] + ain[n, low].astype(F32)).astype(BF16)
        d_low = send(stage.at[n, 1, low], lin.at[n, low], s.at[8], r.at[8], x_right)
        a_high.wait_recv()
        stage[n, 2, high] = (mine[1] + ain[n, high].astype(F32)).astype(BF16)
        d_high = send(stage.at[n, 2, high], rin.at[n, high], s.at[9], r.at[9], x_left)
        for copy in (b_high, b_low, d_low, d_high):
            copy.wait_recv()
        return (
            mine[2] + lin[n, low].astype(F32) + rin[n, low].astype(F32),
            mine[3] + lin[n, high].astype(F32) + rin[n, high].astype(F32),
        )

    def normalize(buf):
        total = jnp.zeros((cap, width), F32)
        for i in range(8):
            total += buf[i].astype(F32)
        mean = jnp.sum(total, axis=1, keepdims=True) * (1.0 / (8 * width))
        square = jnp.zeros((cap, width), F32)
        for i in range(8):
            centered = buf[i].astype(F32) - mean
            square += centered * centered
        var = jnp.sum(square, axis=1, keepdims=True) * (1.0 / (8 * width))
        scale = lax.rsqrt(var + EPS)
        for i in range(8):
            normed[:, i * width : (i + 1) * width] = ((buf[i].astype(F32) - mean) * scale).astype(BF16)

    tokg[mdl] = tok[...]
    gather_tokens = Gather(tokg, 0)
    for h in range(2):
        cols = slice(h * HD, (h + 1) * HD)
        kbuf[0, h] = kc[:, cols]
    k_right = send(kbuf.at[0], kbuf.at[1], kv_s.at[0], kv_r.at[0], y_right)
    k_left = send(kbuf.at[0], kbuf.at[2], kv_s.at[1], kv_r.at[1], y_left)
    for h in range(2):
        cols = slice(h * HD, (h + 1) * HD)
        vtbuf[0, h] = jnp.transpose(vc[:, cols].astype(F32)).astype(BF16)
    v_left = send(vtbuf.at[0], vtbuf.at[2], kv_s.at[2], kv_r.at[2], y_left)
    v_right = send(vtbuf.at[0], vtbuf.at[1], kv_s.at[3], kv_r.at[3], y_right)

    count = lens.shape[1]
    ring = lax.broadcasted_iota(jnp.int32, (8, count), 0)
    ring_device = ((z - ring + NZ) % NZ) * NY + y
    placed = place[...] == ring_device
    held = jnp.where(placed, lens[...], 0).astype(F32)
    upper = (
        lax.broadcasted_iota(jnp.int32, (count, count), 0)
        < lax.broadcasted_iota(jnp.int32, (count, count), 1)
    )
    before = dot(held.astype(BF16), jnp.where(upper, 1.0, 0.0).astype(BF16))
    columns = jnp.transpose(
        jnp.concatenate([before, held, jnp.zeros((count - 16, count), F32)], axis=0)
    )
    row = lax.broadcasted_iota(jnp.int32, (8, count), 0)
    request = lax.broadcasted_iota(jnp.int32, (8, count), 1).astype(F32)
    start_high = jnp.right_shift(start[...], 8).astype(F32)
    start_low = jnp.bitwise_and(start[...], 255).astype(F32)
    values = jnp.where(row == 0, 1.0, 0.0)
    values = jnp.where(row == 1, group[...].astype(F32), values)
    values = jnp.where(row == 2, request, values)
    values = jnp.where(row == 3, start_high, values)
    values = jnp.where(row == 4, start_low, values)
    values = jnp.where(row == 5, jnp.broadcast_to(before[0:1], (8, count)), values)
    values = values.astype(BF16)
    slot = lax.broadcasted_iota(jnp.int32, (count, cap), 1).astype(F32)
    for r in range(NZ):
        first = columns[:, r : r + 1]
        size = columns[:, 8 + r : 9 + r]
        belongs = jnp.where((slot >= first) & (slot < first + size), 1.0, 0.0).astype(BF16)
        table = dot(values, belongs)
        slot_group = jnp.where(table[0:1] > 0.5, table[1:2], -1.0)
        grp_scr[r] = jnp.broadcast_to(slot_group, (8, cap))
        if r == 0:
            own_table = table
    occupied = own_table[0:1]
    slot_request = jnp.where(occupied > 0.5, own_table[2:3], -1.0)
    position = (
        own_table[3:4] * 256.0
        + own_table[4:5]
        + (lax.broadcasted_iota(jnp.int32, (1, cap), 1).astype(F32) - own_table[5:6])
    )
    live = jnp.sum(held[0:1], axis=1, keepdims=True)
    blocks = lax.broadcasted_iota(jnp.int32, (1, owner.shape[1]), 1)
    for b, yb in enumerate((y, yl, yr, ya)):
        mine_block = owner[...] == z * NY + yb
        entry = jnp.where(mine_block, jnp.right_shift(blocks, 3), 0).astype(F32)
        bg_scr[b] = jnp.broadcast_to(jnp.sum(entry, axis=1, keepdims=True), (8, cap))
    pair = lax.broadcasted_iota(jnp.int32, (HD // 2, cap), 0).astype(F32)
    frequency = jnp.exp(pair * (-2.0 * math.log(10000.0) / HD))
    angles = position * frequency
    cosine = jnp.cos(angles)
    sine = jnp.sin(angles)

    gather_tokens.finish()
    normalize(tokg)
    loads[0].wait()

    def rotated(p, h):
        flat = jnp.transpose(dot(normed[...], wqkv_v[p, :, h * HD : (h + 1) * HD]))
        lower, higher = flat[: HD // 2], flat[HD // 2 :]
        return jnp.concatenate(
            [lower * cosine - higher * sine, higher * cosine + lower * sine], axis=0
        )

    factor = math.log2(math.e) * HD ** (-0.5)
    for h in range(2):
        qbuf[0, h] = (rotated(0, h) * factor).astype(BF16)

    q_copies = {}

    def q_step(k):
        for h in range(2):
            if k < 4 or h == 0:
                q_copies[0, k, h] = send(
                    qbuf.at[k - 1, h], qbuf.at[k, h], q_s.at[0, k, h], q_r.at[0, k, h], z_right
                )
            if k < 4 or h == 1:
                q_copies[1, k, h] = send(
                    qbuf.at[(NZ + 1 - k) % NZ, h], qbuf.at[NZ - k, h],
                    q_s.at[1, k, h], q_r.at[1, k, h], z_left,
                )

    def q_wait(k):
        for h in range(2):
            for d in range(2):
                if (d, k, h) in q_copies:
                    q_copies[d, k, h].wait_recv()

    q_step(1)

    for h in range(2):
        kloc[h] = jnp.transpose(rotated(1, h)).astype(BF16)
        vtloc[h] = jnp.transpose(dot(normed[...], wqkv_v[2, :, h * HD : (h + 1) * HD])).astype(BF16)

    k_right.wait_recv()
    fk = send(kbuf.at[1], kbuf.at[3], kv_s.at[4], kv_r.at[4], y_right)
    v_left.wait_recv()
    fv = send(vtbuf.at[2], vtbuf.at[3], kv_s.at[5], kv_r.at[5], y_left)

    def put_stat(ref, top, weight):
        which = lax.broadcasted_iota(jnp.int32, (8, cap), 0)
        ref[...] = jnp.where(which == 0, top, jnp.where(which == 1, weight, 0.0))

    request_column = jnp.transpose(jnp.broadcast_to(slot_request, (HD, cap)))[:, 0:1]
    key_slot = lax.broadcasted_iota(jnp.int32, (cap, cap), 0)
    query_slot = lax.broadcasted_iota(jnp.int32, (cap, cap), 1)
    causal = (request_column == slot_request) & (key_slot <= query_slot) & (slot_request >= 0.0)
    for h in range(2):
        scores = jnp.where(causal, dot(kloc[h], qbuf[0, h]), NEG)
        top = jnp.max(scores, axis=0, keepdims=True)
        weights = jnp.where(causal, jnp.exp2(scores - top), 0.0)
        suf_acc[h] = dot(vtloc[h], weights.astype(BF16))
        put_stat(suf_stat.at[h], top, jnp.sum(weights, axis=0, keepdims=True))

    q_wait(1)
    q_step(2)
    k_left.wait_recv()
    v_right.wait_recv()
    fk.wait_recv()
    fv.wait_recv()

    def attend(r, h):
        query = qbuf[r, h]
        slot_groups = grp_scr[r]
        top = jnp.full((8, cap), NEG, F32)
        for b in range(NY):
            scores = dot(kbuf[b, h], query)
            s_scr[b] = scores
            best = jnp.broadcast_to(jnp.max(scores, axis=0, keepdims=True), (8, cap))
            top = jnp.maximum(top, jnp.where(slot_groups == bg_scr[b], best, NEG))
        total = jnp.zeros((1, cap), F32)
        acc = jnp.zeros((HD, cap), F32)
        for b in range(NY):
            shift = jnp.where(slot_groups == bg_scr[b], top, -NEG)[0:1]
            weights = jnp.exp2(s_scr[b] - shift)
            total += jnp.sum(weights, axis=0, keepdims=True)
            acc += dot(vtbuf[b, h], weights.astype(BF16))
        part_acc[r, h] = acc
        put_stat(part_stat.at[r, h], top[0:1], total)

    def attend_both(k, h):
        def body(i, carry):
            attend(jnp.where(i == 0, k, NZ - k), h)
            return carry

        lax.fori_loop(0, 2, body, 0)

    def attend_heads(r):
        def body(h, carry):
            attend(r, h)
            return carry

        lax.fori_loop(0, 2, body, 0)

    attend_both(1, 0)
    q_wait(2)
    q_step(3)
    attend_both(1, 1)
    attend_both(2, 0)
    q_wait(3)
    q_step(4)
    attend_both(2, 1)
    q_wait(4)
    attend_heads(4)

    def combine(parts):
        top = parts[0][1]
        for part in parts[1:]:
            top = jnp.maximum(top, part[1])
        acc, total = 0.0, 0.0
        for part in parts:
            scale = jnp.exp2(part[1] - top)
            acc = acc + part[0] * scale
            total = total + part[2] * scale
        return acc, top, total

    def own_part(r, h):
        return part_acc[r, h], part_stat[r, h, 0:1], part_stat[r, h, 1:2]

    back = {}

    def arrived(d, k, h):
        for copy in back[d, k, h]:
            copy.wait_recv()
        return rin_acc[d, k, h].astype(F32), rin_stat[d, k, h, 0:1], rin_stat[d, k, h, 1:2]

    def back_step(d, k, h):
        parts = [own_part(NZ - k if d == 0 else k, h)]
        if (d, k + 1, h) in back:
            parts.append(arrived(d, k + 1, h))
        acc, top, total = combine(parts)
        rout_acc[d, k, h] = acc.astype(BF16)
        put_stat(rout_stat.at[d, k, h], top, total)
        device = z_right if d == 0 else z_left
        back[d, k, h] = (
            send(rout_acc.at[d, k, h], rin_acc.at[d, k, h], ra_s.at[d, k, h], ra_r.at[d, k, h], device),
            send(rout_stat.at[d, k, h], rin_stat.at[d, k, h], rs_s.at[d, k, h], rs_r.at[d, k, h], device),
        )

    back_step(0, 4, 0)
    back_step(1, 4, 1)
    attend_both(3, 1)
    back_step(0, 3, 1)
    attend_both(3, 0)
    back_step(1, 3, 0)
    back_step(0, 3, 0)
    back_step(1, 3, 1)
    attend_heads(0)
    for k in (2, 1):
        back_step(0, k, 1)
        back_step(1, k, 0)
        back_step(0, k, 0)
        back_step(1, k, 1)
    rows = []
    for h in range(2):
        suffix = (suf_acc[h], suf_stat[h, 0:1], suf_stat[h, 1:2])
        acc, top, total = combine([own_part(0, h), suffix, arrived(0, 1, h), arrived(1, 1, h)])
        some = total > 0.0
        rows.append(jnp.where(some, acc / jnp.where(some, total, 1.0), 0.0))
    attention = jnp.transpose(jnp.concatenate(rows, axis=0)).astype(BF16)

    loads[1].wait()
    normed[:, 0:width] = attention

    def head_chunk(m):
        return dot(normed[:, 0:width], wo_v[:, pl.ds(pl.multiple_of(m * width, width), width)])

    half = cap // 2
    low, high = reduce_scatter(0, head_chunk)
    resg[mdl, 0:half] = (tok[0:half].astype(F32) + low).astype(BF16)
    resg[mdl, half:cap] = (tok[half:cap].astype(F32) + high).astype(BF16)
    res_own[...] = resg[mdl]

    gather_residual = Gather(resg, 1)
    for load in loads[2:]:
        load.wait()
    gather_residual.finish()
    normalize(resg)
    gate = dot(normed[...], wg_v[...])
    up = dot(normed[...], wu_v[...])
    hidden = (gate / (1.0 + jnp.exp(-gate)) * up).astype(BF16)
    normed[:, 0 : 2 * width] = hidden

    def down_chunk(m):
        return dot(
            normed[:, 0 : 2 * width], wd_v[:, pl.ds(pl.multiple_of(m * width, width), width)]
        )

    low, high = reduce_scatter(1, down_chunk)
    index = lax.broadcasted_iota(jnp.int32, (half, width), 0).astype(F32)
    out[0:half] = jnp.where(index < live, res_own[0:half].astype(F32) + low, 0.0).astype(BF16)
    out[half:cap] = jnp.where(
        index + half < live, res_own[half:cap].astype(F32) + high, 0.0
    ).astype(BF16)
    for copy in pending:
        copy.wait_send()


def local(
    tokens, prefix_cache, qkv_weight, out_weight, gate_up_weight, down_weight,
    lengths, placement, request_group, block_owner, start_position,
):
    cap, width = tokens.shape
    block = prefix_cache.shape[0]
    model = qkv_weight.shape[0]
    hidden = down_weight.shape[0]
    vmem = pl.BlockSpec(memory_space=pltpu.VMEM)
    hbm = pl.BlockSpec(memory_space=pl.ANY)
    dma = pltpu.SemaphoreType.DMA
    ring = (2, 5, 2)
    scratch = [
        pltpu.VMEM((8, cap, width), BF16),
        pltpu.VMEM((8, cap, width), BF16),
        pltpu.VMEM((cap, model), BF16),
        pltpu.VMEM((3, model, width), BF16),
        pltpu.VMEM((width, model), BF16),
        pltpu.VMEM((model, hidden), BF16),
        pltpu.VMEM((model, hidden), BF16),
        pltpu.VMEM((hidden, model), BF16),
        pltpu.VMEM((NY, 2, block, HD), BF16),
        pltpu.VMEM((NY, 2, HD, block), BF16),
        pltpu.VMEM((NZ, 2, HD, cap), BF16),
        pltpu.VMEM((2, cap, HD), BF16),
        pltpu.VMEM((2, HD, cap), BF16),
        pltpu.VMEM((NY, block, cap), F32),
        pltpu.VMEM((NZ, 2, HD, cap), F32),
        pltpu.VMEM((NZ, 2, 8, cap), F32),
        pltpu.VMEM((2, HD, cap), F32),
        pltpu.VMEM((2, 8, cap), F32),
        pltpu.VMEM(ring + (HD, cap), BF16),
        pltpu.VMEM(ring + (8, cap), F32),
        pltpu.VMEM(ring + (HD, cap), BF16),
        pltpu.VMEM(ring + (8, cap), F32),
        pltpu.VMEM((NZ, 8, cap), F32),
        pltpu.VMEM((NY, 8, cap), F32),
        pltpu.VMEM((2, 4, cap, width), BF16),
        pltpu.VMEM((2, 4, cap, width), BF16),
        pltpu.VMEM((2, 3, cap, width), BF16),
        pltpu.VMEM((2, cap, width), BF16),
        pltpu.VMEM((2, cap, width), BF16),
        pltpu.VMEM((2, cap, width), BF16),
        pltpu.VMEM((4, cap // 2, width), F32),
        pltpu.VMEM((cap, width), BF16),
        dma((5,)),
        dma((6,)), dma((6,)),
        dma(ring), dma(ring),
        dma(ring), dma(ring), dma(ring), dma(ring),
        dma((2, 9)), dma((2, 9)), dma((2, 10)), dma((2, 10)),
    ]
    return pl.pallas_call(
        layer_kernel,
        out_shape=jax.ShapeDtypeStruct((cap, width), BF16),
        in_specs=[vmem] * 8 + [hbm] * 5,
        out_specs=vmem,
        scratch_shapes=scratch,
        compiler_params=pltpu.CompilerParams(
            collective_id=0, has_side_effects=True, vmem_limit_bytes=58 << 20
        ),
        name="layer",
    )(
        tokens,
        prefix_cache[:, 0],
        prefix_cache[:, 1],
        lengths.reshape(1, -1),
        placement.reshape(1, -1),
        request_group.reshape(1, -1),
        start_position.reshape(1, -1),
        block_owner.reshape(1, -1),
        jnp.transpose(qkv_weight, (1, 0, 2)),
        out_weight,
        gate_up_weight[:, 0],
        gate_up_weight[:, 1],
        down_weight,
    )


def solution(mesh):
    in_specs = (
        P("req", "mdl"),
        P("req", None, "mdl"),
        P(None, None, "mdl"),
        P("mdl", None),
        P(None, None, "mdl"),
        P("mdl", None),
        P(),
        P(),
        P(),
        P(),
        P(),
    )
    return jax.shard_map(
        local, mesh=mesh, in_specs=in_specs, out_specs=P("req", "mdl"), check_vma=False
    )
```

```python
import functools
import math

import jax
import jax.numpy as jnp
from jax import lax
from jax.experimental import pallas as pl
from jax.experimental.pallas import tpu as pltpu
from jax.sharding import PartitionSpec as P

HD = 128
NEG = -1e30
EPS = 1e-05
NX, NY, NZ = 4, 4, 8
MESH = pl.DeviceIdType.MESH
F32 = jnp.float32
BF16 = jnp.bfloat16


def dot(a, b):
    return jnp.dot(a, b, preferred_element_type=F32)


def layer_kernel(
    tok, lens, place, group, start, owner, cache, wqkv, wo, wgu, wd,
    out,
    tokg, resg, normed, normed_two, att, hid, cache_v, wqkv_v, wo_v, wgu_v, wd_v, wg_v, wu_v,
    kbuf, vtbuf, qbuf, kloc, vtloc, s_scr, part_acc, part_stat, suf_acc, suf_stat,
    rin_acc, rin_stat, rout_acc, rout_stat, grp_scr, bg_scr,
    pair_out, pair_in, stage, landed, mine, res_own,
    wsem, kv_s, kv_r, q_s, q_r, ra_s, ra_r, rs_s, rs_r,
    ag_s, ag_r, sc_s, sc_r,
):
    cap = tok.shape[0]
    width = tok.shape[1]
    req = lax.axis_index("req")
    mdl = lax.axis_index("mdl")
    z = req // NY
    y = req % NY
    x = mdl // 2
    c = mdl % 2
    xr, xl, xa = (x + 1) % NX, (x + NX - 1) % NX, (x + 2) % NX
    yr, yl, ya = (y + 1) % NY, (y + NY - 1) % NY, (y + 2) % NY
    sib = (req, x * 2 + (1 - c))
    x_right = (req, xr * 2 + c)
    x_left = (req, xl * 2 + c)
    x_far = (req, xa * 2 + c)
    y_right = (z * NY + yr, mdl)
    y_left = (z * NY + yl, mdl)
    z_right = ((z + 1) % NZ * NY + y, mdl)
    z_left = ((z + NZ - 1) % NZ * NY + y, mdl)
    pending = []

    def send(src, dst, s_sem, r_sem, device):
        copy = pltpu.make_async_remote_copy(
            src_ref=src, dst_ref=dst, send_sem=s_sem, recv_sem=r_sem,
            device_id=device, device_id_type=MESH,
        )
        copy.start()
        pending.append(copy)
        return copy

    loads = []
    for i, (src, dst) in enumerate(
        (
            (cache.reshape(cache_v.shape), cache_v),
            (wqkv, wqkv_v),
            (wo, wo_v),
            (wgu.reshape(wgu_v.shape), wgu_v),
            (wd, wd_v),
        )
    ):
        load = pltpu.make_async_copy(src, dst, wsem.at[i])
        load.start()
        loads.append(load)

    barrier = pltpu.get_barrier_semaphore()
    for device in (sib, x_right, x_left, x_far, y_right, y_left, z_right, z_left):
        pl.semaphore_signal(barrier, inc=1, device_id=device, device_id_type=MESH)
    pl.semaphore_wait(barrier, 8)

    class Gather:
        def __init__(self, buf, n):
            self.buf = buf
            self.s, self.r = ag_s.at[n], ag_r.at[n]
            own = buf.at[mdl]
            self.direct = [
                send(own, own, self.s.at[i], self.r.at[i], device)
                for i, device in enumerate((x_far, x_right, x_left, sib))
            ]

        def hand_on(self):
            far, right, left, sibling = self.direct
            self.last = [sibling]
            for i, (copy, origin) in enumerate(((right, xl), (left, xr), (far, xa))):
                copy.wait_recv()
                block = self.buf.at[origin * 2 + c]
                self.last.append(send(block, block, self.s.at[4 + i], self.r.at[4 + i], sib))

        def finish(self):
            for copy in self.last:
                copy.wait_recv()

    class Scatter:
        order = ((xa, x_far), (xr, x_right), (xl, x_left), (x, None))

        def __init__(self, n, chunk):
            self.n, self.chunk = n, chunk
            self.s, self.r = sc_s.at[n], sc_r.at[n]
            self.pairs = []
            for i, (xd, device) in enumerate(self.order):
                pair_out[n, i] = chunk(xd * 2 + (1 - c)).astype(BF16)
                self.pairs.append(
                    send(pair_out.at[n, i], pair_in.at[n, i], self.s.at[i], self.r.at[i], sib)
                )

        def cross(self):
            n = self.n
            self.crossed = []
            for i, (xd, device) in enumerate(self.order):
                own = self.chunk(xd * 2 + c)
                self.pairs[i].wait_recv()
                total = own + pair_in[n, i].astype(F32)
                if device is None:
                    mine[n] = total
                else:
                    stage[n, i] = total.astype(BF16)
                    self.crossed.append(
                        send(
                            stage.at[n, i], landed.at[n, i], self.s.at[4 + i], self.r.at[4 + i],
                            device,
                        )
                    )

        def finish(self):
            total = mine[self.n]
            for i, copy in enumerate(self.crossed):
                copy.wait_recv()
                total = total + landed[self.n, i].astype(F32)
            return total

    def normalize(buf, target):
        rows = buf.shape[1]
        total = jnp.zeros((rows, width), F32)
        for i in range(8):
            total += buf[i].astype(F32)
        mean = jnp.sum(total, axis=1, keepdims=True) * (1.0 / (8 * width))
        square = jnp.zeros((rows, width), F32)
        for i in range(8):
            centered = buf[i].astype(F32) - mean
            square += centered * centered
        var = jnp.sum(square, axis=1, keepdims=True) * (1.0 / (8 * width))
        scale = lax.rsqrt(var + EPS)
        for i in range(8):
            target[:, i * width : (i + 1) * width] = (
                (buf[i].astype(F32) - mean) * scale
            ).astype(BF16)

    tokg[mdl] = tok[...]
    gather_tokens = Gather(tokg, 0)
    taken = lax.broadcasted_iota(jnp.int32, (HD, 2 * HD), 1)
    wanted = lax.broadcasted_iota(jnp.int32, (HD, 2 * HD), 0) * 2
    even = jnp.where(taken == wanted, 1.0, 0.0).astype(BF16)
    odd = jnp.where(taken == wanted + 1, 1.0, 0.0).astype(BF16)
    loads[0].wait()
    block = cache_v.shape[0] // 2
    for h in range(2):
        cols = slice(h * HD, (h + 1) * HD)
        for i in range(block // HD):
            rows = slice(i * 2 * HD, (i + 1) * 2 * HD)
            kbuf[0, h, i * HD : (i + 1) * HD] = dot(even, cache_v[rows, cols]).astype(BF16)
    k_right = send(kbuf.at[0], kbuf.at[1], kv_s.at[0], kv_r.at[0], y_right)
    for h in range(2):
        cols = slice(h * HD, (h + 1) * HD)
        for i in range(block // HD):
            rows = slice(i * 2 * HD, (i + 1) * 2 * HD)
            vtbuf[0, h, :, i * HD : (i + 1) * HD] = jnp.transpose(
                dot(odd, cache_v[rows, cols])
            ).astype(BF16)
    v_left = send(vtbuf.at[0], vtbuf.at[2], kv_s.at[2], kv_r.at[2], y_left)

    count = lens.shape[1]
    ring = lax.broadcasted_iota(jnp.int32, (8, count), 0)
    ring_device = ((z - ring + NZ) % NZ) * NY + y
    placed = place[...] == ring_device
    held = jnp.where(placed, lens[...], 0).astype(F32)
    upper = (
        lax.broadcasted_iota(jnp.int32, (count, count), 0)
        < lax.broadcasted_iota(jnp.int32, (count, count), 1)
    )
    before = dot(held.astype(BF16), jnp.where(upper, 1.0, 0.0).astype(BF16))
    columns = jnp.transpose(
        jnp.concatenate([before, held, jnp.zeros((count - 16, count), F32)], axis=0)
    )
    row = lax.broadcasted_iota(jnp.int32, (8, count), 0)
    request = lax.broadcasted_iota(jnp.int32, (8, count), 1).astype(F32)
    start_high = jnp.right_shift(start[...], 8).astype(F32)
    start_low = jnp.bitwise_and(start[...], 255).astype(F32)
    values = jnp.where(row == 0, 1.0, 0.0)
    values = jnp.where(row == 1, group[...].astype(F32), values)
    values = jnp.where(row == 2, request, values)
    values = jnp.where(row == 3, start_high, values)
    values = jnp.where(row == 4, start_low, values)
    values = jnp.where(row == 5, jnp.broadcast_to(before[0:1], (8, count)), values)
    values = values.astype(BF16)
    slot = lax.broadcasted_iota(jnp.int32, (count, cap), 1).astype(F32)
    for r in range(NZ):
        first = columns[:, r : r + 1]
        size = columns[:, 8 + r : 9 + r]
        belongs = jnp.where((slot >= first) & (slot < first + size), 1.0, 0.0).astype(BF16)
        table = dot(values, belongs)
        slot_group = jnp.where(table[0:1] > 0.5, table[1:2], -1.0)
        grp_scr[r] = jnp.broadcast_to(slot_group, (8, cap))
        if r == 0:
            own_table = table
    occupied = own_table[0:1]
    slot_request = jnp.where(occupied > 0.5, own_table[2:3], -1.0)
    position = (
        own_table[3:4] * 256.0
        + own_table[4:5]
        + (lax.broadcasted_iota(jnp.int32, (1, cap), 1).astype(F32) - own_table[5:6])
    )
    live = jnp.sum(held[0:1], axis=1, keepdims=True)
    blocks = lax.broadcasted_iota(jnp.int32, (1, owner.shape[1]), 1)
    for b, yb in enumerate((y, yl, yr, ya)):
        mine_block = owner[...] == z * NY + yb
        entry = jnp.where(mine_block, jnp.right_shift(blocks, 3), 0).astype(F32)
        bg_scr[b] = jnp.broadcast_to(jnp.sum(entry, axis=1, keepdims=True), (8, cap))
    pair = lax.broadcasted_iota(jnp.int32, (HD // 2, cap), 0).astype(F32)
    frequency = jnp.exp(pair * (-2.0 * math.log(10000.0) / HD))
    angles = position * frequency
    cosine = jnp.cos(angles)
    sine = jnp.sin(angles)

    k_right.wait_send()
    k_left = send(kbuf.at[0], kbuf.at[2], kv_s.at[1], kv_r.at[1], y_left)
    v_left.wait_send()
    v_right = send(vtbuf.at[0], vtbuf.at[1], kv_s.at[3], kv_r.at[3], y_right)
    gather_tokens.hand_on()
    k_right.wait_recv()
    fk = send(kbuf.at[1], kbuf.at[3], kv_s.at[4], kv_r.at[4], y_right)
    v_left.wait_recv()
    fv = send(vtbuf.at[2], vtbuf.at[3], kv_s.at[5], kv_r.at[5], y_left)
    gather_tokens.finish()
    normalize(tokg, normed)
    loads[1].wait()

    def rotated(p, h):
        flat = jnp.transpose(dot(normed[...], wqkv_v[p, :, h * HD : (h + 1) * HD]))
        lower, higher = flat[: HD // 2], flat[HD // 2 :]
        return jnp.concatenate(
            [lower * cosine - higher * sine, higher * cosine + lower * sine], axis=0
        )

    factor = math.log2(math.e) * HD ** (-0.5)
    for h in range(2):
        qbuf[0, h] = (rotated(0, h) * factor).astype(BF16)

    q_copies = {}

    def q_send(d, k, h):
        if d == 0:
            source, target, device = qbuf.at[k - 1, h], qbuf.at[k, h], z_right
        else:
            source, target, device = qbuf.at[(NZ + 1 - k) % NZ, h], qbuf.at[NZ - k, h], z_left
        q_copies[d, k, h] = send(source, target, q_s.at[d, k, h], q_r.at[d, k, h], device)

    lanes = ((0, 0), (1, 1), (0, 1), (1, 0))

    def q_pass(k):
        for d, h in lanes:
            if (d, k, h) in q_copies:
                q_copies[d, k, h].wait_recv()
                if k < 3 or (k == 3 and d == h):
                    q_send(d, k + 1, h)

    for d, h in lanes:
        q_send(d, 1, h)

    for h in range(2):
        kloc[h] = jnp.transpose(rotated(1, h)).astype(BF16)
        vtloc[h] = jnp.transpose(dot(normed[...], wqkv_v[2, :, h * HD : (h + 1) * HD])).astype(BF16)

    def put_stat(ref, top, weight):
        which = lax.broadcasted_iota(jnp.int32, (8, cap), 0)
        ref[...] = jnp.where(which == 0, top, jnp.where(which == 1, weight, 0.0))

    request_column = jnp.transpose(jnp.broadcast_to(slot_request, (HD, cap)))[:, 0:1]
    key_slot = lax.broadcasted_iota(jnp.int32, (cap, cap), 0)
    query_slot = lax.broadcasted_iota(jnp.int32, (cap, cap), 1)
    causal = (request_column == slot_request) & (key_slot <= query_slot) & (slot_request >= 0.0)
    for h in range(2):
        scores = jnp.where(causal, dot(kloc[h], qbuf[0, h]), NEG)
        top = jnp.max(scores, axis=0, keepdims=True)
        weights = jnp.where(causal, jnp.exp2(scores - top), 0.0)
        suf_acc[h] = dot(vtloc[h], weights.astype(BF16))
        put_stat(suf_stat.at[h], top, jnp.sum(weights, axis=0, keepdims=True))

    def near_blocks(r, h):
        query = qbuf[r, h]
        slot_groups = grp_scr[r]
        top = jnp.full((8, cap), NEG, F32)
        for b in range(3):
            scores = dot(kbuf[b, h], query)
            s_scr[b] = scores
            best = jnp.broadcast_to(jnp.max(scores, axis=0, keepdims=True), (8, cap))
            top = jnp.maximum(top, jnp.where(slot_groups == bg_scr[b], best, NEG))
        total = jnp.zeros((1, cap), F32)
        acc = jnp.zeros((HD, cap), F32)
        for b in range(3):
            shift = jnp.where(slot_groups == bg_scr[b], top, -NEG)[0:1]
            weights = jnp.exp2(s_scr[b] - shift)
            total += jnp.sum(weights, axis=0, keepdims=True)
            acc += dot(vtbuf[b, h], weights.astype(BF16))
        part_acc[r, h] = acc
        put_stat(part_stat.at[r, h], top[0:1], total)

    def far_block(r, h):
        same = grp_scr[r] == bg_scr[3]
        scores = dot(kbuf[3, h], qbuf[r, h])
        best = jnp.broadcast_to(jnp.max(scores, axis=0, keepdims=True), (8, cap))
        old = part_stat[r, h, 0:1]
        top = jnp.maximum(old, jnp.where(same, best, NEG)[0:1])
        weights = jnp.exp2(scores - jnp.where(same[0:1], top, -NEG))
        scale = jnp.exp2(old - top)
        total = part_stat[r, h, 1:2] * scale + jnp.sum(weights, axis=0, keepdims=True)
        acc = part_acc[r, h] * scale + dot(vtbuf[3, h], weights.astype(BF16))
        part_acc[r, h] = acc
        put_stat(part_stat.at[r, h], top, total)

    def for_both(k, step):
        def body(i, carry):
            step(jnp.where(i < 2, k, NZ - k), i % 2)
            return carry

        lax.fori_loop(0, 4, body, 0)

    def for_heads(r, step):
        def body(h, carry):
            step(r, h)
            return carry

        lax.fori_loop(0, 2, body, 0)

    q_pass(1)
    k_left.wait_recv()
    v_right.wait_recv()
    for_heads(0, near_blocks)
    q_pass(2)
    for_both(1, near_blocks)
    q_pass(3)
    for_both(2, near_blocks)
    q_pass(4)
    for_heads(4, near_blocks)
    fk.wait_recv()
    fv.wait_recv()

    def combine(parts):
        top = parts[0][1]
        for part in parts[1:]:
            top = jnp.maximum(top, part[1])
        acc, total = 0.0, 0.0
        for part in parts:
            scale = jnp.exp2(part[1] - top)
            acc = acc + part[0] * scale
            total = total + part[2] * scale
        return acc, top, total

    back = {}

    def own_part(r, h):
        return part_acc[r, h], part_stat[r, h, 0:1], part_stat[r, h, 1:2]

    def arrived(d, k, h):
        for copy in back[d, k, h]:
            copy.wait_recv()
        return rin_acc[d, k, h].astype(F32), rin_stat[d, k, h, 0:1], rin_stat[d, k, h, 1:2]

    def back_step(d, k, h):
        parts = [own_part(NZ - k if d == 0 else k, h)]
        if (d, k + 1, h) in back:
            parts.append(arrived(d, k + 1, h))
        acc, top, total = combine(parts)
        rout_acc[d, k, h] = acc.astype(BF16)
        put_stat(rout_stat.at[d, k, h], top, total)
        device = z_right if d == 0 else z_left
        back[d, k, h] = (
            send(rout_acc.at[d, k, h], rin_acc.at[d, k, h], ra_s.at[d, k, h], ra_r.at[d, k, h], device),
            send(rout_stat.at[d, k, h], rin_stat.at[d, k, h], rs_s.at[d, k, h], rs_r.at[d, k, h], device),
        )

    far_block(4, 0)
    back_step(0, 4, 0)
    far_block(4, 1)
    back_step(1, 4, 1)
    for_both(3, near_blocks)
    for_both(3, far_block)
    for d, h in ((0, 1), (1, 0), (0, 0), (1, 1)):
        back_step(d, 3, h)
    for_both(2, far_block)
    for d, h in lanes:
        back_step(d, 2, h)
    for_both(1, far_block)
    for d, h in lanes:
        back_step(d, 1, h)
    for_heads(0, far_block)
    rows = []
    for h in range(2):
        parts = [
            (suf_acc[h], suf_stat[h, 0:1], suf_stat[h, 1:2]),
            (part_acc[0, h], part_stat[0, h, 0:1], part_stat[0, h, 1:2]),
        ]
        parts += [arrived(0, 1, h), arrived(1, 1, h)]
        acc, top, total = combine(parts)
        some = total > 0.0
        rows.append(jnp.where(some, acc / jnp.where(some, total, 1.0), 0.0))
    attention = jnp.transpose(jnp.concatenate(rows, axis=0)).astype(BF16)

    half = cap // 2
    halves = (0, 1)
    for i in halves:
        att[i] = attention[i * half : (i + 1) * half]
    loads[2].wait()

    def columns_of(weight, m):
        return weight[:, pl.ds(pl.multiple_of(m * width, width), width)]

    scatters = [Scatter(i, lambda m, i=i: dot(att[i], columns_of(wo_v, m))) for i in halves]
    for scatter in scatters:
        scatter.cross()
    loads[3].wait()
    loads[4].wait()

    def split(i, carry):
        pairs = wgu_v[pl.ds(i * 2 * HD, 2 * HD)]
        wg_v[pl.ds(i * HD, HD)] = dot(even, pairs).astype(BF16)
        wu_v[pl.ds(i * HD, HD)] = dot(odd, pairs).astype(BF16)
        return carry

    lax.fori_loop(0, wg_v.shape[0] // HD, split, 0)
    gathers = []
    for i in halves:
        own = tok[i * half : (i + 1) * half].astype(F32) + scatters[i].finish()
        resg[i, mdl] = own.astype(BF16)
        res_own[i] = own.astype(BF16)
        gathers.append(Gather(resg.at[i], 1 + i))
    for gather in gathers:
        gather.hand_on()
    scatters = []
    for i in halves:
        gathers[i].finish()
        normalize(resg.at[i], normed_two.at[i])
        gate = dot(normed_two[i], wg_v[...])
        up = dot(normed_two[i], wu_v[...])
        hid[i] = (gate / (1.0 + jnp.exp(-gate)) * up).astype(BF16)
        scatters.append(Scatter(2 + i, lambda m, i=i: dot(hid[i], columns_of(wd_v, m))))
    for scatter in scatters:
        scatter.cross()
    index = lax.broadcasted_iota(jnp.int32, (half, width), 0).astype(F32)
    for i in halves:
        finished = res_own[i].astype(F32) + scatters[i].finish()
        out[i * half : (i + 1) * half] = jnp.where(
            index + float(i * half) < live, finished, 0.0
        ).astype(BF16)
    for copy in pending:
        if copy is not k_right and copy is not v_left:
            copy.wait_send()


def local(
    tokens, prefix_cache, qkv_weight, out_weight, gate_up_weight, down_weight,
    lengths, placement, request_group, block_owner, start_position,
):
    cap, width = tokens.shape
    block = prefix_cache.shape[0]
    model = qkv_weight.shape[0]
    hidden = down_weight.shape[0]
    vmem = pl.BlockSpec(memory_space=pltpu.VMEM)
    hbm = pl.BlockSpec(memory_space=pl.ANY)
    dma = pltpu.SemaphoreType.DMA
    half = cap // 2
    ring = (2, 5, 2)
    scratch = [
        pltpu.VMEM((8, cap, width), BF16),
        pltpu.VMEM((2, 8, half, width), BF16),
        pltpu.VMEM((cap, model), BF16),
        pltpu.VMEM((2, half, model), BF16),
        pltpu.VMEM((2, half, width), BF16),
        pltpu.VMEM((2, half, hidden), BF16),
        pltpu.VMEM((2 * block, width), BF16),
        pltpu.VMEM((3, model, width), BF16),
        pltpu.VMEM((width, model), BF16),
        pltpu.VMEM((2 * model, hidden), BF16),
        pltpu.VMEM((hidden, model), BF16),
        pltpu.VMEM((model, hidden), BF16),
        pltpu.VMEM((model, hidden), BF16),
        pltpu.VMEM((NY, 2, block, HD), BF16),
        pltpu.VMEM((NY, 2, HD, block), BF16),
        pltpu.VMEM((NZ, 2, HD, cap), BF16),
        pltpu.VMEM((2, cap, HD), BF16),
        pltpu.VMEM((2, HD, cap), BF16),
        pltpu.VMEM((3, block, cap), F32),
        pltpu.VMEM((NZ, 2, HD, cap), F32),
        pltpu.VMEM((NZ, 2, 8, cap), F32),
        pltpu.VMEM((2, HD, cap), F32),
        pltpu.VMEM((2, 8, cap), F32),
        pltpu.VMEM(ring + (HD, cap), BF16),
        pltpu.VMEM(ring + (8, cap), F32),
        pltpu.VMEM(ring + (HD, cap), BF16),
        pltpu.VMEM(ring + (8, cap), F32),
        pltpu.VMEM((NZ, 8, cap), F32),
        pltpu.VMEM((NY, 8, cap), F32),
        pltpu.VMEM((4, 4, half, width), BF16),
        pltpu.VMEM((4, 4, half, width), BF16),
        pltpu.VMEM((4, 3, half, width), BF16),
        pltpu.VMEM((4, 3, half, width), BF16),
        pltpu.VMEM((4, half, width), F32),
        pltpu.VMEM((2, half, width), BF16),
        dma((5,)),
        dma((6,)), dma((6,)),
        dma(ring), dma(ring),
        dma(ring), dma(ring), dma(ring), dma(ring),
        dma((3, 7)), dma((3, 7)), dma((4, 7)), dma((4, 7)),
    ]
    return pl.pallas_call(
        layer_kernel,
        out_shape=jax.ShapeDtypeStruct((cap, width), BF16),
        in_specs=[vmem] * 6 + [hbm] * 5,
        out_specs=vmem,
        scratch_shapes=scratch,
        compiler_params=pltpu.CompilerParams(
            collective_id=0, has_side_effects=True, vmem_limit_bytes=58 << 20
        ),
        name="layer",
    )(
        tokens,
        lengths.reshape(1, -1),
        placement.reshape(1, -1),
        request_group.reshape(1, -1),
        start_position.reshape(1, -1),
        block_owner.reshape(1, -1),
        prefix_cache,
        jnp.transpose(qkv_weight, (1, 0, 2)),
        out_weight,
        gate_up_weight,
        down_weight,
    )


def solution(mesh):
    in_specs = (
        P("req", "mdl"),
        P("req", None, "mdl"),
        P(None, None, "mdl"),
        P("mdl", None),
        P(None, None, "mdl"),
        P("mdl", None),
        P(),
        P(),
        P(),
        P(),
        P(),
    )
    return jax.shard_map(
        local, mesh=mesh, in_specs=in_specs, out_specs=P("req", "mdl"), check_vma=False
    )
```

```python
import functools
import math

import jax
import jax.numpy as jnp
from jax import lax
from jax.experimental import pallas as pl
from jax.experimental.pallas import tpu as pltpu
from jax.sharding import PartitionSpec as P

HD = 128
NEG = -1e30
EPS = 1e-05
NX, NY, NZ = 4, 4, 8
MESH = pl.DeviceIdType.MESH
F32 = jnp.float32
BF16 = jnp.bfloat16


def dot(a, b):
    return jnp.dot(a, b, preferred_element_type=F32)


def layer_kernel(
    tok, lens, place, group, start, owner, cache, wqkv, wo, wgu, wd,
    out,
    tokg, resg, normed, normed_two, att, hid, cache_v, wqkv_v, wo_v, wgu_v, wd_v, wg_v, wu_v,
    kbuf, vtbuf, qbuf, kloc, vtloc, s_scr, part_acc, part_stat, suf_acc, suf_stat,
    rin_acc, rin_stat, rout_acc, rout_stat, grp_scr, bg_scr,
    pair_out, pair_in, stage, landed, mine, res_own,
    wsem, kv_s, kv_r, q_s, q_r, ra_s, ra_r, rs_s, rs_r,
    ag_s, ag_r, sc_s, sc_r,
):
    cap = tok.shape[0]
    width = tok.shape[1]
    req = lax.axis_index("req")
    mdl = lax.axis_index("mdl")
    z = req // NY
    y = req % NY
    x = mdl // 2
    c = mdl % 2
    xr, xl, xa = (x + 1) % NX, (x + NX - 1) % NX, (x + 2) % NX
    yr, yl, ya = (y + 1) % NY, (y + NY - 1) % NY, (y + 2) % NY
    sib = (req, x * 2 + (1 - c))
    x_right = (req, xr * 2 + c)
    x_left = (req, xl * 2 + c)
    x_far = (req, xa * 2 + c)
    y_right = (z * NY + yr, mdl)
    y_left = (z * NY + yl, mdl)
    z_right = ((z + 1) % NZ * NY + y, mdl)
    z_left = ((z + NZ - 1) % NZ * NY + y, mdl)
    pending = []

    def send(src, dst, s_sem, r_sem, device):
        copy = pltpu.make_async_remote_copy(
            src_ref=src, dst_ref=dst, send_sem=s_sem, recv_sem=r_sem,
            device_id=device, device_id_type=MESH,
        )
        copy.start()
        pending.append(copy)
        return copy

    loads = []
    for i, (src, dst) in enumerate(
        (
            (cache.reshape(cache_v.shape), cache_v),
            (wqkv, wqkv_v),
            (wo, wo_v),
            (wgu.reshape(wgu_v.shape), wgu_v),
            (wd, wd_v),
        )
    ):
        load = pltpu.make_async_copy(src, dst, wsem.at[i])
        load.start()
        loads.append(load)

    barrier = pltpu.get_barrier_semaphore()
    for device in (sib, x_right, x_left, x_far, y_right, y_left, z_right, z_left):
        pl.semaphore_signal(barrier, inc=1, device_id=device, device_id_type=MESH)
    pl.semaphore_wait(barrier, 8)

    class Gather:
        def __init__(self, buf, n):
            self.buf = buf
            self.s, self.r = ag_s.at[n], ag_r.at[n]
            own = buf.at[mdl]
            self.direct = [
                send(own, own, self.s.at[i], self.r.at[i], device)
                for i, device in enumerate((x_right, x_left, sib, x_far))
            ]

        def hand_on(self):
            right, left, sibling, far = self.direct
            self.last = [sibling]
            for i, (copy, origin) in enumerate(((right, xl), (left, xr), (far, xa))):
                copy.wait_recv()
                block = self.buf.at[origin * 2 + c]
                self.last.append(send(block, block, self.s.at[4 + i], self.r.at[4 + i], sib))

        def finish(self):
            for copy in self.last:
                copy.wait_recv()

    class Scatter:
        order = ((xr, x_right), (xl, x_left), (xa, x_far), (x, None))

        def __init__(self, n, chunk):
            self.n, self.chunk = n, chunk
            self.s, self.r = sc_s.at[n], sc_r.at[n]
            self.pairs = []
            for i, (xd, device) in enumerate(self.order):
                pair_out[n, i] = chunk(xd * 2 + (1 - c)).astype(BF16)
                self.pairs.append(
                    send(pair_out.at[n, i], pair_in.at[n, i], self.s.at[i], self.r.at[i], sib)
                )

        def cross(self):
            n = self.n
            self.crossed = []
            for i, (xd, device) in enumerate(self.order):
                own = self.chunk(xd * 2 + c)
                self.pairs[i].wait_recv()
                total = own + pair_in[n, i].astype(F32)
                if device is None:
                    mine[n] = total
                else:
                    stage[n, i] = total.astype(BF16)
                    self.crossed.append(
                        send(
                            stage.at[n, i], landed.at[n, i], self.s.at[4 + i], self.r.at[4 + i],
                            device,
                        )
                    )

        def finish(self):
            total = mine[self.n]
            for i, copy in enumerate(self.crossed):
                copy.wait_recv()
                total = total + landed[self.n, i].astype(F32)
            return total

    def normalize(buf, target):
        rows = buf.shape[1]
        total = jnp.zeros((rows, width), F32)
        for i in range(8):
            total += buf[i].astype(F32)
        mean = jnp.sum(total, axis=1, keepdims=True) * (1.0 / (8 * width))
        square = jnp.zeros((rows, width), F32)
        for i in range(8):
            centered = buf[i].astype(F32) - mean
            square += centered * centered
        var = jnp.sum(square, axis=1, keepdims=True) * (1.0 / (8 * width))
        scale = lax.rsqrt(var + EPS)
        for i in range(8):
            target[:, i * width : (i + 1) * width] = (
                (buf[i].astype(F32) - mean) * scale
            ).astype(BF16)

    tokg[mdl] = tok[...]
    gather_tokens = Gather(tokg, 0)
    taken = lax.broadcasted_iota(jnp.int32, (HD, 2 * HD), 1)
    wanted = lax.broadcasted_iota(jnp.int32, (HD, 2 * HD), 0) * 2
    even = jnp.where(taken == wanted, 1.0, 0.0).astype(BF16)
    odd = jnp.where(taken == wanted + 1, 1.0, 0.0).astype(BF16)
    loads[0].wait()
    block = cache_v.shape[0] // 2
    for h in range(2):
        cols = slice(h * HD, (h + 1) * HD)
        for i in range(block // HD):
            rows = slice(i * 2 * HD, (i + 1) * 2 * HD)
            kbuf[0, h, i * HD : (i + 1) * HD] = dot(even, cache_v[rows, cols]).astype(BF16)
    k_right = send(kbuf.at[0], kbuf.at[1], kv_s.at[0], kv_r.at[0], y_right)
    for h in range(2):
        cols = slice(h * HD, (h + 1) * HD)
        for i in range(block // HD):
            rows = slice(i * 2 * HD, (i + 1) * 2 * HD)
            vtbuf[0, h, :, i * HD : (i + 1) * HD] = jnp.transpose(
                dot(odd, cache_v[rows, cols])
            ).astype(BF16)
    v_left = send(vtbuf.at[0], vtbuf.at[2], kv_s.at[2], kv_r.at[2], y_left)

    count = lens.shape[1]
    ring = lax.broadcasted_iota(jnp.int32, (8, count), 0)
    ring_device = ((z - ring + NZ) % NZ) * NY + y
    placed = place[...] == ring_device
    held = jnp.where(placed, lens[...], 0).astype(F32)
    upper = (
        lax.broadcasted_iota(jnp.int32, (count, count), 0)
        < lax.broadcasted_iota(jnp.int32, (count, count), 1)
    )
    before = dot(held.astype(BF16), jnp.where(upper, 1.0, 0.0).astype(BF16))
    columns = jnp.transpose(
        jnp.concatenate([before, held, jnp.zeros((count - 16, count), F32)], axis=0)
    )
    row = lax.broadcasted_iota(jnp.int32, (8, count), 0)
    request = lax.broadcasted_iota(jnp.int32, (8, count), 1).astype(F32)
    start_high = jnp.right_shift(start[...], 8).astype(F32)
    start_low = jnp.bitwise_and(start[...], 255).astype(F32)
    values = jnp.where(row == 0, 1.0, 0.0)
    values = jnp.where(row == 1, group[...].astype(F32), values)
    values = jnp.where(row == 2, request, values)
    values = jnp.where(row == 3, start_high, values)
    values = jnp.where(row == 4, start_low, values)
    values = jnp.where(row == 5, jnp.broadcast_to(before[0:1], (8, count)), values)
    values = values.astype(BF16)
    slot = lax.broadcasted_iota(jnp.int32, (count, cap), 1).astype(F32)
    for r in range(NZ):
        first = columns[:, r : r + 1]
        size = columns[:, 8 + r : 9 + r]
        belongs = jnp.where((slot >= first) & (slot < first + size), 1.0, 0.0).astype(BF16)
        table = dot(values, belongs)
        slot_group = jnp.where(table[0:1] > 0.5, table[1:2], -1.0)
        grp_scr[r] = jnp.broadcast_to(slot_group, (8, cap))
        if r == 0:
            own_table = table
    occupied = own_table[0:1]
    slot_request = jnp.where(occupied > 0.5, own_table[2:3], -1.0)
    position = (
        own_table[3:4] * 256.0
        + own_table[4:5]
        + (lax.broadcasted_iota(jnp.int32, (1, cap), 1).astype(F32) - own_table[5:6])
    )
    live = jnp.sum(held[0:1], axis=1, keepdims=True)
    blocks = lax.broadcasted_iota(jnp.int32, (1, owner.shape[1]), 1)
    for b, yb in enumerate((y, yl, yr, ya)):
        mine_block = owner[...] == z * NY + yb
        entry = jnp.where(mine_block, jnp.right_shift(blocks, 3), 0).astype(F32)
        bg_scr[b] = jnp.broadcast_to(jnp.sum(entry, axis=1, keepdims=True), (8, cap))
    pair = lax.broadcasted_iota(jnp.int32, (HD // 2, cap), 0).astype(F32)
    frequency = jnp.exp(pair * (-2.0 * math.log(10000.0) / HD))
    angles = position * frequency
    cosine = jnp.cos(angles)
    sine = jnp.sin(angles)

    k_right.wait_send()
    k_left = send(kbuf.at[0], kbuf.at[2], kv_s.at[1], kv_r.at[1], y_left)
    v_left.wait_send()
    v_right = send(vtbuf.at[0], vtbuf.at[1], kv_s.at[3], kv_r.at[3], y_right)
    gather_tokens.hand_on()
    k_right.wait_recv()
    fk = send(kbuf.at[1], kbuf.at[3], kv_s.at[4], kv_r.at[4], y_right)
    v_left.wait_recv()
    fv = send(vtbuf.at[2], vtbuf.at[3], kv_s.at[5], kv_r.at[5], y_left)
    gather_tokens.finish()
    normalize(tokg, normed)
    loads[1].wait()

    def rotated(p, h):
        flat = jnp.transpose(dot(normed[...], wqkv_v[p, :, h * HD : (h + 1) * HD]))
        lower, higher = flat[: HD // 2], flat[HD // 2 :]
        return jnp.concatenate(
            [lower * cosine - higher * sine, higher * cosine + lower * sine], axis=0
        )

    factor = math.log2(math.e) * HD ** (-0.5)
    for h in range(2):
        qbuf[0, h] = (rotated(0, h) * factor).astype(BF16)

    q_copies = {}

    def q_send(d, k, h):
        if d == 0:
            source, target, device = qbuf.at[k - 1, h], qbuf.at[k, h], z_right
        else:
            source, target, device = qbuf.at[(NZ + 1 - k) % NZ, h], qbuf.at[NZ - k, h], z_left
        q_copies[d, k, h] = send(source, target, q_s.at[d, k, h], q_r.at[d, k, h], device)

    lanes = ((0, 0), (1, 1), (0, 1), (1, 0))

    def q_pass(k):
        for d, h in lanes:
            if (d, k, h) in q_copies:
                q_copies[d, k, h].wait_recv()
                if k < 3 or (k == 3 and d == h):
                    q_send(d, k + 1, h)

    for d, h in lanes:
        q_send(d, 1, h)

    def put_stat(ref, top, weight):
        which = lax.broadcasted_iota(jnp.int32, (8, cap), 0)
        ref[...] = jnp.where(which == 0, top, jnp.where(which == 1, weight, 0.0))

    def near_blocks(r, h):
        query = qbuf[r, h]
        slot_groups = grp_scr[r]
        top = jnp.full((8, cap), NEG, F32)
        for b in range(3):
            scores = dot(kbuf[b, h], query)
            s_scr[b] = scores
            best = jnp.broadcast_to(jnp.max(scores, axis=0, keepdims=True), (8, cap))
            top = jnp.maximum(top, jnp.where(slot_groups == bg_scr[b], best, NEG))
        total = jnp.zeros((1, cap), F32)
        acc = jnp.zeros((HD, cap), F32)
        for b in range(3):
            shift = jnp.where(slot_groups == bg_scr[b], top, -NEG)[0:1]
            weights = jnp.exp2(s_scr[b] - shift)
            total += jnp.sum(weights, axis=0, keepdims=True)
            acc += dot(vtbuf[b, h], weights.astype(BF16))
        part_acc[r, h] = acc
        put_stat(part_stat.at[r, h], top[0:1], total)

    def far_block(r, h):
        same = grp_scr[r] == bg_scr[3]
        scores = dot(kbuf[3, h], qbuf[r, h])
        best = jnp.broadcast_to(jnp.max(scores, axis=0, keepdims=True), (8, cap))
        old = part_stat[r, h, 0:1]
        top = jnp.maximum(old, jnp.where(same, best, NEG)[0:1])
        weights = jnp.exp2(scores - jnp.where(same[0:1], top, -NEG))
        scale = jnp.exp2(old - top)
        total = part_stat[r, h, 1:2] * scale + jnp.sum(weights, axis=0, keepdims=True)
        acc = part_acc[r, h] * scale + dot(vtbuf[3, h], weights.astype(BF16))
        part_acc[r, h] = acc
        put_stat(part_stat.at[r, h], top, total)

    def for_both(k, step):
        def body(i, carry):
            step(jnp.where(i < 2, k, NZ - k), i % 2)
            return carry

        lax.fori_loop(0, 4, body, 0)

    def for_heads(r, step):
        def body(h, carry):
            step(r, h)
            return carry

        lax.fori_loop(0, 2, body, 0)

    q_pass(1)
    k_left.wait_recv()
    v_right.wait_recv()
    for_heads(0, near_blocks)
    q_pass(2)
    for_both(1, near_blocks)
    q_pass(3)
    for_both(2, near_blocks)
    q_pass(4)
    for_heads(4, near_blocks)
    fk.wait_recv()
    fv.wait_recv()

    def combine(parts):
        top = parts[0][1]
        for part in parts[1:]:
            top = jnp.maximum(top, part[1])
        acc, total = 0.0, 0.0
        for part in parts:
            scale = jnp.exp2(part[1] - top)
            acc = acc + part[0] * scale
            total = total + part[2] * scale
        return acc, top, total

    back = {}

    def own_part(r, h):
        return part_acc[r, h], part_stat[r, h, 0:1], part_stat[r, h, 1:2]

    def arrived(d, k, h):
        for copy in back[d, k, h]:
            copy.wait_recv()
        return rin_acc[d, k, h].astype(F32), rin_stat[d, k, h, 0:1], rin_stat[d, k, h, 1:2]

    def back_step(d, k, h):
        parts = [own_part(NZ - k if d == 0 else k, h)]
        if (d, k + 1, h) in back:
            parts.append(arrived(d, k + 1, h))
        acc, top, total = combine(parts)
        rout_acc[d, k, h] = acc.astype(BF16)
        put_stat(rout_stat.at[d, k, h], top, total)
        device = z_right if d == 0 else z_left
        back[d, k, h] = (
            send(rout_acc.at[d, k, h], rin_acc.at[d, k, h], ra_s.at[d, k, h], ra_r.at[d, k, h], device),
            send(rout_stat.at[d, k, h], rin_stat.at[d, k, h], rs_s.at[d, k, h], rs_r.at[d, k, h], device),
        )

    far_block(4, 0)
    back_step(0, 4, 0)
    far_block(4, 1)
    back_step(1, 4, 1)
    for_both(3, near_blocks)
    for_both(3, far_block)
    for d, h in ((0, 1), (1, 0), (0, 0), (1, 1)):
        back_step(d, 3, h)
    for_both(2, far_block)
    for d, h in lanes:
        back_step(d, 2, h)
    for_both(1, far_block)
    for d, h in lanes:
        back_step(d, 1, h)
    for_heads(0, far_block)

    for h in range(2):
        kloc[h] = jnp.transpose(rotated(1, h)).astype(BF16)
        vtloc[h] = jnp.transpose(dot(normed[...], wqkv_v[2, :, h * HD : (h + 1) * HD])).astype(BF16)

    request_column = jnp.transpose(jnp.broadcast_to(slot_request, (HD, cap)))[:, 0:1]
    key_slot = lax.broadcasted_iota(jnp.int32, (cap, cap), 0)
    query_slot = lax.broadcasted_iota(jnp.int32, (cap, cap), 1)
    causal = (request_column == slot_request) & (key_slot <= query_slot) & (slot_request >= 0.0)
    for h in range(2):
        scores = jnp.where(causal, dot(kloc[h], qbuf[0, h]), NEG)
        top = jnp.max(scores, axis=0, keepdims=True)
        weights = jnp.where(causal, jnp.exp2(scores - top), 0.0)
        suf_acc[h] = dot(vtloc[h], weights.astype(BF16))
        put_stat(suf_stat.at[h], top, jnp.sum(weights, axis=0, keepdims=True))

    rows = []
    for h in range(2):
        parts = [
            (suf_acc[h], suf_stat[h, 0:1], suf_stat[h, 1:2]),
            (part_acc[0, h], part_stat[0, h, 0:1], part_stat[0, h, 1:2]),
        ]
        parts += [arrived(0, 1, h), arrived(1, 1, h)]
        acc, top, total = combine(parts)
        some = total > 0.0
        rows.append(jnp.where(some, acc / jnp.where(some, total, 1.0), 0.0))
    attention = jnp.transpose(jnp.concatenate(rows, axis=0)).astype(BF16)

    half = cap // 2
    halves = (0, 1)
    for i in halves:
        att[i] = attention[i * half : (i + 1) * half]
    loads[2].wait()

    def columns_of(weight, m):
        return weight[:, pl.ds(pl.multiple_of(m * width, width), width)]

    scatters = [Scatter(i, lambda m, i=i: dot(att[i], columns_of(wo_v, m))) for i in halves]
    for scatter in scatters:
        scatter.cross()
    loads[3].wait()
    loads[4].wait()

    def split(i, carry):
        pairs = wgu_v[pl.ds(i * 2 * HD, 2 * HD)]
        wg_v[pl.ds(i * HD, HD)] = dot(even, pairs).astype(BF16)
        wu_v[pl.ds(i * HD, HD)] = dot(odd, pairs).astype(BF16)
        return carry

    lax.fori_loop(0, wg_v.shape[0] // HD, split, 0)
    gathers = []
    for i in halves:
        own = tok[i * half : (i + 1) * half].astype(F32) + scatters[i].finish()
        resg[i, mdl] = own.astype(BF16)
        res_own[i] = own.astype(BF16)
        gathers.append(Gather(resg.at[i], 1 + i))
    for gather in gathers:
        gather.hand_on()
    scatters = []
    for i in halves:
        gathers[i].finish()
        normalize(resg.at[i], normed_two.at[i])
        gate = dot(normed_two[i], wg_v[...])
        up = dot(normed_two[i], wu_v[...])
        hid[i] = (gate / (1.0 + jnp.exp(-gate)) * up).astype(BF16)
        scatters.append(Scatter(2 + i, lambda m, i=i: dot(hid[i], columns_of(wd_v, m))))
    for scatter in scatters:
        scatter.cross()
    index = lax.broadcasted_iota(jnp.int32, (half, width), 0).astype(F32)
    for i in halves:
        finished = res_own[i].astype(F32) + scatters[i].finish()
        out[i * half : (i + 1) * half] = jnp.where(
            index + float(i * half) < live, finished, 0.0
        ).astype(BF16)
    for copy in pending:
        if copy is not k_right and copy is not v_left:
            copy.wait_send()


def local(
    tokens, prefix_cache, qkv_weight, out_weight, gate_up_weight, down_weight,
    lengths, placement, request_group, block_owner, start_position,
):
    cap, width = tokens.shape
    block = prefix_cache.shape[0]
    model = qkv_weight.shape[0]
    hidden = down_weight.shape[0]
    vmem = pl.BlockSpec(memory_space=pltpu.VMEM)
    hbm = pl.BlockSpec(memory_space=pl.ANY)
    dma = pltpu.SemaphoreType.DMA
    half = cap // 2
    ring = (2, 5, 2)
    scratch = [
        pltpu.VMEM((8, cap, width), BF16),
        pltpu.VMEM((2, 8, half, width), BF16),
        pltpu.VMEM((cap, model), BF16),
        pltpu.VMEM((2, half, model), BF16),
        pltpu.VMEM((2, half, width), BF16),
        pltpu.VMEM((2, half, hidden), BF16),
        pltpu.VMEM((2 * block, width), BF16),
        pltpu.VMEM((3, model, width), BF16),
        pltpu.VMEM((width, model), BF16),
        pltpu.VMEM((2 * model, hidden), BF16),
        pltpu.VMEM((hidden, model), BF16),
        pltpu.VMEM((model, hidden), BF16),
        pltpu.VMEM((model, hidden), BF16),
        pltpu.VMEM((NY, 2, block, HD), BF16),
        pltpu.VMEM((NY, 2, HD, block), BF16),
        pltpu.VMEM((NZ, 2, HD, cap), BF16),
        pltpu.VMEM((2, cap, HD), BF16),
        pltpu.VMEM((2, HD, cap), BF16),
        pltpu.VMEM((3, block, cap), F32),
        pltpu.VMEM((NZ, 2, HD, cap), F32),
        pltpu.VMEM((NZ, 2, 8, cap), F32),
        pltpu.VMEM((2, HD, cap), F32),
        pltpu.VMEM((2, 8, cap), F32),
        pltpu.VMEM(ring + (HD, cap), BF16),
        pltpu.VMEM(ring + (8, cap), F32),
        pltpu.VMEM(ring + (HD, cap), BF16),
        pltpu.VMEM(ring + (8, cap), F32),
        pltpu.VMEM((NZ, 8, cap), F32),
        pltpu.VMEM((NY, 8, cap), F32),
        pltpu.VMEM((4, 4, half, width), BF16),
        pltpu.VMEM((4, 4, half, width), BF16),
        pltpu.VMEM((4, 3, half, width), BF16),
        pltpu.VMEM((4, 3, half, width), BF16),
        pltpu.VMEM((4, half, width), F32),
        pltpu.VMEM((2, half, width), BF16),
        dma((5,)),
        dma((6,)), dma((6,)),
        dma(ring), dma(ring),
        dma(ring), dma(ring), dma(ring), dma(ring),
        dma((3, 7)), dma((3, 7)), dma((4, 7)), dma((4, 7)),
    ]
    return pl.pallas_call(
        layer_kernel,
        out_shape=jax.ShapeDtypeStruct((cap, width), BF16),
        in_specs=[vmem] * 6 + [hbm] * 5,
        out_specs=vmem,
        scratch_shapes=scratch,
        compiler_params=pltpu.CompilerParams(
            collective_id=0, has_side_effects=True, vmem_limit_bytes=58 << 20
        ),
        name="layer",
    )(
        tokens,
        lengths.reshape(1, -1),
        placement.reshape(1, -1),
        request_group.reshape(1, -1),
        start_position.reshape(1, -1),
        block_owner.reshape(1, -1),
        prefix_cache,
        jnp.transpose(qkv_weight, (1, 0, 2)),
        out_weight,
        gate_up_weight,
        down_weight,
    )


def solution(mesh):
    in_specs = (
        P("req", "mdl"),
        P("req", None, "mdl"),
        P(None, None, "mdl"),
        P("mdl", None),
        P(None, None, "mdl"),
        P("mdl", None),
        P(),
        P(),
        P(),
        P(),
        P(),
    )
    return jax.shard_map(
        local, mesh=mesh, in_specs=in_specs, out_specs=P("req", "mdl"), check_vma=False
    )
```

```python
import functools
import math

import jax
import jax.numpy as jnp
from jax import lax
from jax.experimental import pallas as pl
from jax.experimental.pallas import tpu as pltpu
from jax.sharding import PartitionSpec as P

HD = 128
NEG = -1e30
EPS = 1e-05
NX, NY, NZ = 4, 4, 8
MESH = pl.DeviceIdType.MESH
F32 = jnp.float32
BF16 = jnp.bfloat16


def dot(a, b):
    return jnp.dot(a, b, preferred_element_type=F32)


def layer_kernel(
    tok, lens, place, group, start, owner, cache, wqkv, wo, wgu, wd,
    out,
    tokg, resg, normed, normed_two, att, hid, cache_v, wqkv_v, wo_v, wgu_v, wd_v, wg_v, wu_v,
    kbuf, vtbuf, qbuf, kloc, vtloc, s_scr, part_acc, part_stat, suf_acc, suf_stat,
    rin_acc, rin_stat, rout_acc, rout_stat, grp_scr, bg_scr,
    pair_out, pair_in, stage, landed, mine, res_own,
    wsem, kv_s, kv_r, q_s, q_r, ra_s, ra_r, rs_s, rs_r,
    ag_s, ag_r, sc_s, sc_r,
):
    cap = tok.shape[0]
    width = tok.shape[1]
    req = lax.axis_index("req")
    mdl = lax.axis_index("mdl")
    z = req // NY
    y = req % NY
    x = mdl // 2
    c = mdl % 2
    xr, xl, xa = (x + 1) % NX, (x + NX - 1) % NX, (x + 2) % NX
    yr, yl, ya = (y + 1) % NY, (y + NY - 1) % NY, (y + 2) % NY
    sib = (req, x * 2 + (1 - c))
    x_right = (req, xr * 2 + c)
    x_left = (req, xl * 2 + c)
    x_far = (req, xa * 2 + c)
    y_right = (z * NY + yr, mdl)
    y_left = (z * NY + yl, mdl)
    z_right = ((z + 1) % NZ * NY + y, mdl)
    z_left = ((z + NZ - 1) % NZ * NY + y, mdl)
    pending = []

    def send(src, dst, s_sem, r_sem, device):
        copy = pltpu.make_async_remote_copy(
            src_ref=src, dst_ref=dst, send_sem=s_sem, recv_sem=r_sem,
            device_id=device, device_id_type=MESH,
        )
        copy.start()
        pending.append(copy)
        return copy

    loads = []
    for i, (src, dst) in enumerate(
        (
            (cache.reshape(cache_v.shape), cache_v),
            (wqkv, wqkv_v),
            (wo, wo_v),
            (wgu.reshape(wgu_v.shape), wgu_v),
            (wd, wd_v),
        )
    ):
        load = pltpu.make_async_copy(src, dst, wsem.at[i])
        load.start()
        loads.append(load)

    barrier = pltpu.get_barrier_semaphore()
    for device in (sib, x_right, x_left, x_far, y_right, y_left, z_right, z_left):
        pl.semaphore_signal(barrier, inc=1, device_id=device, device_id_type=MESH)
    pl.semaphore_wait(barrier, 8)

    class Gather:
        def __init__(self, buf, n):
            self.buf = buf
            self.s, self.r = ag_s.at[n], ag_r.at[n]
            own = buf.at[mdl]
            self.direct = [
                send(own, own, self.s.at[i], self.r.at[i], device)
                for i, device in enumerate((x_right, x_left, sib, x_far))
            ]

        def hand_on(self):
            right, left, sibling, far = self.direct
            self.last = [sibling]
            for i, (copy, origin) in enumerate(((right, xl), (left, xr), (far, xa))):
                copy.wait_recv()
                block = self.buf.at[origin * 2 + c]
                self.last.append(send(block, block, self.s.at[4 + i], self.r.at[4 + i], sib))

        def finish(self):
            for copy in self.last:
                copy.wait_recv()

    class Scatter:
        order = ((xr, x_right), (xl, x_left), (xa, x_far), (x, None))

        def __init__(self, n, chunk):
            self.n, self.chunk = n, chunk
            self.s, self.r = sc_s.at[n], sc_r.at[n]
            self.pairs = []
            for i, (xd, device) in enumerate(self.order):
                pair_out[n, i] = chunk(xd * 2 + (1 - c)).astype(BF16)
                self.pairs.append(
                    send(pair_out.at[n, i], pair_in.at[n, i], self.s.at[i], self.r.at[i], sib)
                )

        def cross(self):
            n = self.n
            self.crossed = []
            for i, (xd, device) in enumerate(self.order):
                own = self.chunk(xd * 2 + c)
                self.pairs[i].wait_recv()
                total = own + pair_in[n, i].astype(F32)
                if device is None:
                    mine[n] = total
                else:
                    stage[n, i] = total.astype(BF16)
                    self.crossed.append(
                        send(
                            stage.at[n, i], landed.at[n, i], self.s.at[4 + i], self.r.at[4 + i],
                            device,
                        )
                    )

        def finish(self):
            total = mine[self.n]
            for i, copy in enumerate(self.crossed):
                copy.wait_recv()
                total = total + landed[self.n, i].astype(F32)
            return total

    def normalize(buf, target):
        rows = buf.shape[1]
        total = jnp.zeros((rows, width), F32)
        for i in range(8):
            total += buf[i].astype(F32)
        mean = jnp.sum(total, axis=1, keepdims=True) * (1.0 / (8 * width))
        square = jnp.zeros((rows, width), F32)
        for i in range(8):
            centered = buf[i].astype(F32) - mean
            square += centered * centered
        var = jnp.sum(square, axis=1, keepdims=True) * (1.0 / (8 * width))
        scale = lax.rsqrt(var + EPS)
        for i in range(8):
            target[:, i * width : (i + 1) * width] = (
                (buf[i].astype(F32) - mean) * scale
            ).astype(BF16)

    tokg[mdl] = tok[...]
    gather_tokens = Gather(tokg, 0)
    taken = lax.broadcasted_iota(jnp.int32, (HD, 2 * HD), 1)
    wanted = lax.broadcasted_iota(jnp.int32, (HD, 2 * HD), 0) * 2
    even = jnp.where(taken == wanted, 1.0, 0.0).astype(BF16)
    odd = jnp.where(taken == wanted + 1, 1.0, 0.0).astype(BF16)
    loads[0].wait()
    block = cache_v.shape[0] // 2
    for h in range(2):
        cols = slice(h * HD, (h + 1) * HD)
        for i in range(block // HD):
            rows = slice(i * 2 * HD, (i + 1) * 2 * HD)
            kbuf[0, h, i * HD : (i + 1) * HD] = dot(even, cache_v[rows, cols]).astype(BF16)
    k_right = send(kbuf.at[0], kbuf.at[1], kv_s.at[0], kv_r.at[0], y_right)
    for h in range(2):
        cols = slice(h * HD, (h + 1) * HD)
        for i in range(block // HD):
            rows = slice(i * 2 * HD, (i + 1) * 2 * HD)
            vtbuf[0, h, :, i * HD : (i + 1) * HD] = jnp.transpose(
                dot(odd, cache_v[rows, cols])
            ).astype(BF16)
    v_left = send(vtbuf.at[0], vtbuf.at[2], kv_s.at[2], kv_r.at[2], y_left)

    count = lens.shape[1]
    ring = lax.broadcasted_iota(jnp.int32, (8, count), 0)
    ring_device = ((z - ring + NZ) % NZ) * NY + y
    placed = place[...] == ring_device
    held = jnp.where(placed, lens[...], 0).astype(F32)
    upper = (
        lax.broadcasted_iota(jnp.int32, (count, count), 0)
        < lax.broadcasted_iota(jnp.int32, (count, count), 1)
    )
    before = dot(held.astype(BF16), jnp.where(upper, 1.0, 0.0).astype(BF16))
    columns = jnp.transpose(
        jnp.concatenate([before, held, jnp.zeros((count - 16, count), F32)], axis=0)
    )
    row = lax.broadcasted_iota(jnp.int32, (8, count), 0)
    request = lax.broadcasted_iota(jnp.int32, (8, count), 1).astype(F32)
    start_high = jnp.right_shift(start[...], 8).astype(F32)
    start_low = jnp.bitwise_and(start[...], 255).astype(F32)
    values = jnp.where(row == 0, 1.0, 0.0)
    values = jnp.where(row == 1, group[...].astype(F32), values)
    values = jnp.where(row == 2, request, values)
    values = jnp.where(row == 3, start_high, values)
    values = jnp.where(row == 4, start_low, values)
    values = jnp.where(row == 5, jnp.broadcast_to(before[0:1], (8, count)), values)
    values = values.astype(BF16)
    slot = lax.broadcasted_iota(jnp.int32, (count, cap), 1).astype(F32)
    for r in range(NZ):
        first = columns[:, r : r + 1]
        size = columns[:, 8 + r : 9 + r]
        belongs = jnp.where((slot >= first) & (slot < first + size), 1.0, 0.0).astype(BF16)
        table = dot(values, belongs)
        slot_group = jnp.where(table[0:1] > 0.5, table[1:2], -1.0)
        grp_scr[r] = jnp.broadcast_to(slot_group, (8, cap))
        if r == 0:
            own_table = table
    occupied = own_table[0:1]
    slot_request = jnp.where(occupied > 0.5, own_table[2:3], -1.0)
    position = (
        own_table[3:4] * 256.0
        + own_table[4:5]
        + (lax.broadcasted_iota(jnp.int32, (1, cap), 1).astype(F32) - own_table[5:6])
    )
    live = jnp.sum(held[0:1], axis=1, keepdims=True)
    blocks = lax.broadcasted_iota(jnp.int32, (1, owner.shape[1]), 1)
    for b, yb in enumerate((y, yl, yr, ya)):
        mine_block = owner[...] == z * NY + yb
        entry = jnp.where(mine_block, jnp.right_shift(blocks, 3), 0).astype(F32)
        bg_scr[b] = jnp.broadcast_to(jnp.sum(entry, axis=1, keepdims=True), (8, cap))
    pair = lax.broadcasted_iota(jnp.int32, (HD // 2, cap), 0).astype(F32)
    frequency = jnp.exp(pair * (-2.0 * math.log(10000.0) / HD))
    angles = position * frequency
    cosine = jnp.cos(angles)
    sine = jnp.sin(angles)

    k_right.wait_send()
    k_left = send(kbuf.at[0], kbuf.at[2], kv_s.at[1], kv_r.at[1], y_left)
    v_left.wait_send()
    v_right = send(vtbuf.at[0], vtbuf.at[1], kv_s.at[3], kv_r.at[3], y_right)
    gather_tokens.hand_on()
    k_right.wait_recv()
    fk = send(kbuf.at[1], kbuf.at[3], kv_s.at[4], kv_r.at[4], y_right)
    v_left.wait_recv()
    fv = send(vtbuf.at[2], vtbuf.at[3], kv_s.at[5], kv_r.at[5], y_left)
    gather_tokens.finish()
    normalize(tokg, normed)
    loads[1].wait()

    def rotated(p, h):
        flat = jnp.transpose(dot(normed[...], wqkv_v[p, :, h * HD : (h + 1) * HD]))
        lower, higher = flat[: HD // 2], flat[HD // 2 :]
        return jnp.concatenate(
            [lower * cosine - higher * sine, higher * cosine + lower * sine], axis=0
        )

    factor = math.log2(math.e) * HD ** (-0.5)
    for h in range(2):
        qbuf[0, h] = (rotated(0, h) * factor).astype(BF16)

    q_copies = {}

    def q_send(d, k, h):
        if d == 0:
            source, target, device = qbuf.at[k - 1, h], qbuf.at[k, h], z_right
        else:
            source, target, device = qbuf.at[(NZ + 1 - k) % NZ, h], qbuf.at[NZ - k, h], z_left
        q_copies[d, k, h] = send(source, target, q_s.at[d, k, h], q_r.at[d, k, h], device)

    lanes = ((0, 0), (1, 1), (0, 1), (1, 0))

    def q_pass(k):
        for d, h in lanes:
            if (d, k, h) in q_copies:
                q_copies[d, k, h].wait_recv()
                if k < 3 or (k == 3 and d == h):
                    q_send(d, k + 1, h)

    for d, h in lanes:
        q_send(d, 1, h)

    def put_stat(ref, top, weight):
        which = lax.broadcasted_iota(jnp.int32, (8, cap), 0)
        ref[...] = jnp.where(which == 0, top, jnp.where(which == 1, weight, 0.0))

    def near_blocks(r, h):
        query = qbuf[r, h]
        slot_groups = grp_scr[r]
        top = jnp.full((8, cap), NEG, F32)
        for b in range(3):
            scores = dot(kbuf[b, h], query)
            s_scr[b] = scores
            best = jnp.broadcast_to(jnp.max(scores, axis=0, keepdims=True), (8, cap))
            top = jnp.maximum(top, jnp.where(slot_groups == bg_scr[b], best, NEG))
        total = jnp.zeros((1, cap), F32)
        acc = jnp.zeros((HD, cap), F32)
        for b in range(3):
            shift = jnp.where(slot_groups == bg_scr[b], top, -NEG)[0:1]
            weights = jnp.exp2(s_scr[b] - shift)
            total += jnp.sum(weights, axis=0, keepdims=True)
            acc += dot(vtbuf[b, h], weights.astype(BF16))
        part_acc[r, h] = acc
        put_stat(part_stat.at[r, h], top[0:1], total)

    def far_block(r, h):
        same = grp_scr[r] == bg_scr[3]
        scores = dot(kbuf[3, h], qbuf[r, h])
        best = jnp.broadcast_to(jnp.max(scores, axis=0, keepdims=True), (8, cap))
        old = part_stat[r, h, 0:1]
        top = jnp.maximum(old, jnp.where(same, best, NEG)[0:1])
        weights = jnp.exp2(scores - jnp.where(same[0:1], top, -NEG))
        scale = jnp.exp2(old - top)
        total = part_stat[r, h, 1:2] * scale + jnp.sum(weights, axis=0, keepdims=True)
        acc = part_acc[r, h] * scale + dot(vtbuf[3, h], weights.astype(BF16))
        part_acc[r, h] = acc
        put_stat(part_stat.at[r, h], top, total)

    def for_both(k, step):
        def body(i, carry):
            step(jnp.where(i < 2, k, NZ - k), i % 2)
            return carry

        lax.fori_loop(0, 4, body, 0)

    def for_one(k, h, step):
        def body(i, carry):
            step(jnp.where(i == 0, k, NZ - k), h)
            return carry

        lax.fori_loop(0, 2, body, 0)

    def for_heads(r, step):
        def body(h, carry):
            step(r, h)
            return carry

        lax.fori_loop(0, 2, body, 0)

    q_pass(1)
    k_left.wait_recv()
    v_right.wait_recv()
    for_heads(0, near_blocks)
    q_pass(2)
    for_both(1, near_blocks)
    q_pass(3)
    for_both(3, near_blocks)
    q_pass(4)
    for_heads(4, near_blocks)
    fk.wait_recv()
    fv.wait_recv()

    def combine(parts):
        top = parts[0][1]
        for part in parts[1:]:
            top = jnp.maximum(top, part[1])
        acc, total = 0.0, 0.0
        for part in parts:
            scale = jnp.exp2(part[1] - top)
            acc = acc + part[0] * scale
            total = total + part[2] * scale
        return acc, top, total

    back = {}

    def own_part(r, h):
        return part_acc[r, h], part_stat[r, h, 0:1], part_stat[r, h, 1:2]

    def arrived(d, k, h):
        for copy in back[d, k, h]:
            copy.wait_recv()
        return rin_acc[d, k, h].astype(F32), rin_stat[d, k, h, 0:1], rin_stat[d, k, h, 1:2]

    def back_step(d, k, h):
        parts = [own_part(NZ - k if d == 0 else k, h)]
        if (d, k + 1, h) in back:
            parts.append(arrived(d, k + 1, h))
        acc, top, total = combine(parts)
        rout_acc[d, k, h] = acc.astype(BF16)
        put_stat(rout_stat.at[d, k, h], top, total)
        device = z_right if d == 0 else z_left
        back[d, k, h] = (
            send(rout_acc.at[d, k, h], rin_acc.at[d, k, h], ra_s.at[d, k, h], ra_r.at[d, k, h], device),
            send(rout_stat.at[d, k, h], rin_stat.at[d, k, h], rs_s.at[d, k, h], rs_r.at[d, k, h], device),
        )

    far_block(4, 0)
    back_step(0, 4, 0)
    far_block(4, 1)
    back_step(1, 4, 1)
    for_both(3, far_block)
    back_step(0, 3, 1)
    back_step(1, 3, 0)
    for_one(2, 0, near_blocks)
    back_step(0, 3, 0)
    back_step(1, 3, 1)
    for_one(2, 1, near_blocks)
    for_both(2, far_block)
    for d, h in lanes:
        back_step(d, 2, h)
    for_both(1, far_block)
    for d, h in lanes:
        back_step(d, 1, h)
    for_heads(0, far_block)

    for h in range(2):
        kloc[h] = jnp.transpose(rotated(1, h)).astype(BF16)
        vtloc[h] = jnp.transpose(dot(normed[...], wqkv_v[2, :, h * HD : (h + 1) * HD])).astype(BF16)

    request_column = jnp.transpose(jnp.broadcast_to(slot_request, (HD, cap)))[:, 0:1]
    key_slot = lax.broadcasted_iota(jnp.int32, (cap, cap), 0)
    query_slot = lax.broadcasted_iota(jnp.int32, (cap, cap), 1)
    causal = (request_column == slot_request) & (key_slot <= query_slot) & (slot_request >= 0.0)
    for h in range(2):
        scores = jnp.where(causal, dot(kloc[h], qbuf[0, h]), NEG)
        top = jnp.max(scores, axis=0, keepdims=True)
        weights = jnp.where(causal, jnp.exp2(scores - top), 0.0)
        suf_acc[h] = dot(vtloc[h], weights.astype(BF16))
        put_stat(suf_stat.at[h], top, jnp.sum(weights, axis=0, keepdims=True))

    rows = []
    for h in range(2):
        parts = [
            (suf_acc[h], suf_stat[h, 0:1], suf_stat[h, 1:2]),
            (part_acc[0, h], part_stat[0, h, 0:1], part_stat[0, h, 1:2]),
        ]
        parts += [arrived(0, 1, h), arrived(1, 1, h)]
        acc, top, total = combine(parts)
        some = total > 0.0
        rows.append(jnp.where(some, acc / jnp.where(some, total, 1.0), 0.0))
    attention = jnp.transpose(jnp.concatenate(rows, axis=0)).astype(BF16)

    half = cap // 2
    halves = (0, 1)
    for i in halves:
        att[i] = attention[i * half : (i + 1) * half]
    loads[2].wait()

    def columns_of(weight, m):
        return weight[:, pl.ds(pl.multiple_of(m * width, width), width)]

    scatters = [Scatter(i, lambda m, i=i: dot(att[i], columns_of(wo_v, m))) for i in halves]
    for scatter in scatters:
        scatter.cross()
    loads[3].wait()
    loads[4].wait()

    def split(i, carry):
        pairs = wgu_v[pl.ds(i * 2 * HD, 2 * HD)]
        wg_v[pl.ds(i * HD, HD)] = dot(even, pairs).astype(BF16)
        wu_v[pl.ds(i * HD, HD)] = dot(odd, pairs).astype(BF16)
        return carry

    lax.fori_loop(0, wg_v.shape[0] // HD, split, 0)
    gathers = []
    for i in halves:
        own = tok[i * half : (i + 1) * half].astype(F32) + scatters[i].finish()
        resg[i, mdl] = own.astype(BF16)
        res_own[i] = own.astype(BF16)
        gathers.append(Gather(resg.at[i], 1 + i))
    for gather in gathers:
        gather.hand_on()
    scatters = []
    for i in halves:
        gathers[i].finish()
        normalize(resg.at[i], normed_two.at[i])
        gate = dot(normed_two[i], wg_v[...])
        up = dot(normed_two[i], wu_v[...])
        hid[i] = (gate / (1.0 + jnp.exp(-gate)) * up).astype(BF16)
        scatters.append(Scatter(2 + i, lambda m, i=i: dot(hid[i], columns_of(wd_v, m))))
    for scatter in scatters:
        scatter.cross()
    index = lax.broadcasted_iota(jnp.int32, (half, width), 0).astype(F32)
    for i in halves:
        finished = res_own[i].astype(F32) + scatters[i].finish()
        out[i * half : (i + 1) * half] = jnp.where(
            index + float(i * half) < live, finished, 0.0
        ).astype(BF16)
    for copy in pending:
        if copy is not k_right and copy is not v_left:
            copy.wait_send()


def local(
    tokens, prefix_cache, qkv_weight, out_weight, gate_up_weight, down_weight,
    lengths, placement, request_group, block_owner, start_position,
):
    cap, width = tokens.shape
    block = prefix_cache.shape[0]
    model = qkv_weight.shape[0]
    hidden = down_weight.shape[0]
    vmem = pl.BlockSpec(memory_space=pltpu.VMEM)
    hbm = pl.BlockSpec(memory_space=pl.ANY)
    dma = pltpu.SemaphoreType.DMA
    half = cap // 2
    ring = (2, 5, 2)
    scratch = [
        pltpu.VMEM((8, cap, width), BF16),
        pltpu.VMEM((2, 8, half, width), BF16),
        pltpu.VMEM((cap, model), BF16),
        pltpu.VMEM((2, half, model), BF16),
        pltpu.VMEM((2, half, width), BF16),
        pltpu.VMEM((2, half, hidden), BF16),
        pltpu.VMEM((2 * block, width), BF16),
        pltpu.VMEM((3, model, width), BF16),
        pltpu.VMEM((width, model), BF16),
        pltpu.VMEM((2 * model, hidden), BF16),
        pltpu.VMEM((hidden, model), BF16),
        pltpu.VMEM((model, hidden), BF16),
        pltpu.VMEM((model, hidden), BF16),
        pltpu.VMEM((NY, 2, block, HD), BF16),
        pltpu.VMEM((NY, 2, HD, block), BF16),
        pltpu.VMEM((NZ, 2, HD, cap), BF16),
        pltpu.VMEM((2, cap, HD), BF16),
        pltpu.VMEM((2, HD, cap), BF16),
        pltpu.VMEM((3, block, cap), F32),
        pltpu.VMEM((NZ, 2, HD, cap), F32),
        pltpu.VMEM((NZ, 2, 8, cap), F32),
        pltpu.VMEM((2, HD, cap), F32),
        pltpu.VMEM((2, 8, cap), F32),
        pltpu.VMEM(ring + (HD, cap), BF16),
        pltpu.VMEM(ring + (8, cap), F32),
        pltpu.VMEM(ring + (HD, cap), BF16),
        pltpu.VMEM(ring + (8, cap), F32),
        pltpu.VMEM((NZ, 8, cap), F32),
        pltpu.VMEM((NY, 8, cap), F32),
        pltpu.VMEM((4, 4, half, width), BF16),
        pltpu.VMEM((4, 4, half, width), BF16),
        pltpu.VMEM((4, 3, half, width), BF16),
        pltpu.VMEM((4, 3, half, width), BF16),
        pltpu.VMEM((4, half, width), F32),
        pltpu.VMEM((2, half, width), BF16),
        dma((5,)),
        dma((6,)), dma((6,)),
        dma(ring), dma(ring),
        dma(ring), dma(ring), dma(ring), dma(ring),
        dma((3, 7)), dma((3, 7)), dma((4, 7)), dma((4, 7)),
    ]
    return pl.pallas_call(
        layer_kernel,
        out_shape=jax.ShapeDtypeStruct((cap, width), BF16),
        in_specs=[vmem] * 6 + [hbm] * 5,
        out_specs=vmem,
        scratch_shapes=scratch,
        compiler_params=pltpu.CompilerParams(
            collective_id=0, has_side_effects=True, vmem_limit_bytes=58 << 20
        ),
        name="layer",
    )(
        tokens,
        lengths.reshape(1, -1),
        placement.reshape(1, -1),
        request_group.reshape(1, -1),
        start_position.reshape(1, -1),
        block_owner.reshape(1, -1),
        prefix_cache,
        jnp.transpose(qkv_weight, (1, 0, 2)),
        out_weight,
        gate_up_weight,
        down_weight,
    )


def solution(mesh):
    in_specs = (
        P("req", "mdl"),
        P("req", None, "mdl"),
        P(None, None, "mdl"),
        P("mdl", None),
        P(None, None, "mdl"),
        P("mdl", None),
        P(),
        P(),
        P(),
        P(),
        P(),
    )
    return jax.shard_map(
        local, mesh=mesh, in_specs=in_specs, out_specs=P("req", "mdl"), check_vma=False
    )
```
